128 devices in a mesh: gx: 16 (over z, x_hi, core), gy: 8 (over x_lo, y).
Axes of the slice: x: 4 (x_hi: 2, x_lo: 2; x = x_hi * 2 + x_lo), y: 4, z: 4, core: 2. Of those that a mesh axis runs over, the one named last changes fastest.
Arguments:
- right_side: float32 [2, 2, 256, 128, 128], P(None, None, 'gx', 'gy'), may hold values from -7 to 7
- slowness: float32 [256, 128, 128], P('gx', 'gy'), may hold values from 0.7 to 1.4
- source_cells: int32 [2, 16], replicated, may hold values from 0 to 4194303
- source_amplitudes: float32 [2, 16, 2], replicated, may hold values from -24 to 24
Outputs:
- wavefield: float32 [2, 2, 256, 128, 128], P(None, None, 'gx', 'gy')
- residual: float32 [2, 2, 256, 128, 128], P(None, None, 'gx', 'gy')
The draws below stay inside these ranges and needn't reach their ends.
Inputs may be any that keep to these rules, and one draw needn't show every extreme that they name: `source_cells`: flat indices (x * 128 + y) * 128 + z of cells; points may coincide.
All inputs are finite; a program needn't handle non-finite values.
Results may differ from the reference program's by a relative error of at most 0.0003.
Values sent between devices are 32-bit elements; how exact they have to be, the bound alone decides.
A program may use at most 64 MiB of HBM per device.

```python
import math
import jax
import jax.numpy as jnp
from jax import lax

CX = 16
CY = 16
NZ = 128
NRHS = 2
NPT = 16
NX = 256
NY = 128
N_GX = 16
N_GY = 8


def draw_right_side(key, part):
    random_part = jnp.clip(jax.random.normal(key, (NRHS, 2, NX, NY, NZ), jnp.float32), -6.0, 6.0)
    return random_part


def plant(drawn, stream_key, smallest, largest):
    spot = [jax.random.randint(jax.random.fold_in(stream_key, axis), (), 0, length) for axis, length in enumerate(drawn.shape)]
    widest = drawn.shape.index(max(drawn.shape))
    neighbour = spot[:widest] + [(spot[widest] + 1) % drawn.shape[widest]] + spot[widest + 1:]
    return drawn.at[tuple(spot)].set(smallest).at[tuple(neighbour)].set(largest)


def levels(own_key, extent, pieces, least, largest):
    def one(dim, parts):
        draws = jax.random.uniform(jax.random.fold_in(jax.random.fold_in(own_key, 6), dim), (parts,), jnp.float32, least / len(pieces), largest / len(pieces))
        return jnp.repeat(jnp.exp(draws), extent[dim] // parts).reshape((-1,) + (1,) * (len(extent) - dim - 1))

    level = one(*pieces[0])
    for cut in pieces[1:]:
        level = level * one(*cut)
    return level


def centred(rng, shape, deviation, limit, kind=jnp.bfloat16):
    values = jax.random.normal(rng, shape, jnp.float32) * deviation
    return jnp.minimum(jnp.maximum(values, -limit), limit).astype(kind)


def setup_inputs(seed: int = 0) -> dict:
    splits = jax.random.split(jax.random.key(seed), 5)
    right_side = draw_right_side(jax.random.fold_in(splits[4], 71), 0)
    slowness = jnp.clip(jnp.exp(math.log(1.4) - 0.6931472 * jax.random.uniform(splits[1], (NX, NY, NZ), jnp.float32) ** levels(splits[1], (NX, NY, NZ), ((0, 16), (1, 8)), -0.2, 0.2)), 0.7, 1.4)
    source_cells = plant(jax.random.randint(splits[2], (NRHS, NPT), 0, NX * NY * NZ), jax.random.fold_in(splits[2], 1), 0, (NX * NY * NZ) - 1).astype(jnp.int32)
    source_amplitudes = centred(splits[3], (NRHS, NPT, 2), 4.0, 24.0, jnp.float32)
    return {"right_side": right_side, "slowness": slowness, "source_cells": source_cells, "source_amplitudes": source_amplitudes}


KAPPA = 0.12
DAMPING = 0.3
HIGHEST = lax.Precision.HIGHEST

def sine_basis(length):
    positions = jnp.arange(1, length + 1).astype(jnp.float32)
    angles = positions * (math.pi / (length + 1))
    sine_rows = math.sqrt(2.0 / (length + 1)) * jnp.sin(angles[:, None] * positions[None, :])
    return (sine_rows, angles)

def build_tables(size_x, size_y, cells_z):
    sine_x, angle_x = sine_basis(size_x)
    sine_y, angle_y = sine_basis(size_y)
    sine_z, angle_z = sine_basis(cells_z)
    symbol_x = 2.5 - 8.0 / 3.0 * jnp.cos(angle_x) + 1.0 / 6.0 * jnp.cos(2.0 * angle_x)
    symbol_y = 2.5 - 8.0 / 3.0 * jnp.cos(angle_y) + 1.0 / 6.0 * jnp.cos(2.0 * angle_y)
    symbol_z = 2.0 - 2.0 * jnp.cos(angle_z)
    real_part = symbol_x[:, None, None] + symbol_y[None, :, None] + symbol_z[None, None, :] - KAPPA
    denominator = real_part * real_part + (KAPPA * DAMPING) ** 2
    return (sine_x, sine_y, sine_z, real_part / denominator, KAPPA * DAMPING / denominator)

def transform(wavefield, sine_x, sine_y, sine_z):
    result = jnp.einsum('scxyz,zw->scxyw', wavefield, sine_z, precision=HIGHEST)
    result = jnp.einsum('scxyz,xa->scayz', result, sine_x, precision=HIGHEST)
    return jnp.einsum('scxyz,yb->scxbz', result, sine_y, precision=HIGHEST)

def fast_solve(wavefield, tables):
    sine_x, sine_y, sine_z, inverse_real, inverse_imag = tables
    spectrum = transform(wavefield, sine_x, sine_y, sine_z)
    real_part = inverse_real * spectrum[:, 0] - inverse_imag * spectrum[:, 1]
    imag_part = inverse_real * spectrum[:, 1] + inverse_imag * spectrum[:, 0]
    return transform(jnp.stack([real_part, imag_part], axis=1), sine_x, sine_y, sine_z)

def apply_operator(padded, slowness):
    size_x = padded.shape[2] - 4
    size_y = padded.shape[3] - 4
    center = padded[:, :, 2:2 + size_x, 2:2 + size_y]
    weights = (1.0, -16.0, 30.0, -16.0, 1.0)
    lateral = jnp.zeros_like(center)
    for offset in range(5):
        lateral = lateral + weights[offset] / 12.0 * (padded[:, :, offset:offset + size_x, 2:2 + size_y] + padded[:, :, 2:2 + size_x, offset:offset + size_y])
    vertical = jnp.pad(center, ((0, 0), (0, 0), (0, 0), (0, 0), (1, 1)))
    lateral = lateral + 2.0 * center - vertical[..., :-2] - vertical[..., 2:]
    scaled = KAPPA * slowness
    real_part = lateral[:, 0] - scaled * (center[:, 0] - DAMPING * center[:, 1])
    imag_part = lateral[:, 1] - scaled * (center[:, 1] + DAMPING * center[:, 0])
    return jnp.stack([real_part, imag_part], axis=1)

def tile_solve(source_term, trace_x, trace_y, slowness, tables):
    source_term = source_term.at[:, :, 0].add((16.0 * trace_x[:, :, 1] - trace_x[:, :, 0]) / 12.0)
    source_term = source_term.at[:, :, 1].add(-trace_x[:, :, 1] / 12.0)
    source_term = source_term.at[:, :, :, 0].add((16.0 * trace_y[:, :, :, 1] - trace_y[:, :, :, 0]) / 12.0)
    source_term = source_term.at[:, :, :, 1].add(-trace_y[:, :, :, 1] / 12.0)
    wavefield = fast_solve(source_term, tables)
    for sweep_step in range(2):
        padded = jnp.pad(wavefield, ((0, 0), (0, 0), (2, 2), (2, 2), (0, 0)))
        wavefield = wavefield + fast_solve(source_term - apply_operator(padded, slowness), tables)
    return wavefield

def point_sources(flat_cells, amplitudes, start_x, start_y, size_x, size_y, cells_z, total_y):
    plane_cells = total_y * cells_z
    coord_x = flat_cells // plane_cells - start_x
    coord_y = flat_cells // cells_z % total_y - start_y
    coord_z = flat_cells % cells_z
    match_x = (coord_x[:, :, None] == jnp.arange(size_x, dtype=jnp.int32)[None, None, :]).astype(jnp.float32)
    match_y = (coord_y[:, :, None] == jnp.arange(size_y, dtype=jnp.int32)[None, None, :]).astype(jnp.float32)
    match_z = (coord_z[:, :, None] == jnp.arange(cells_z, dtype=jnp.int32)[None, None, :]).astype(jnp.float32)
    return jnp.einsum('spc,spx,spy,spz->scxyz', amplitudes, match_x, match_y, match_z, precision=HIGHEST)

def reference(right_side, slowness, source_cells, source_amplitudes):
    forcing = right_side + point_sources(source_cells, source_amplitudes, 0, 0, NX, NY, NZ, NY)
    tables = build_tables(CX, CY, NZ)
    visit_order = sorted(((grid_row + grid_col, grid_row, grid_col) for grid_row in range(N_GX) for grid_col in range(N_GY)))
    tile_rows = jnp.array([triple[1] for triple in visit_order], dtype=jnp.int32)
    tile_cols = jnp.array([triple[2] for triple in visit_order], dtype=jnp.int32)
    anchor = jnp.int32(0)

    def visit(position, wavefield):
        start_x = (tile_rows[position] * CX).astype(jnp.int32)
        start_y = (tile_cols[position] * CY).astype(jnp.int32)
        padded = jnp.pad(wavefield, ((0, 0), (0, 0), (2, 0), (2, 0), (0, 0)))
        trace_x = lax.dynamic_slice(padded, (anchor, anchor, start_x, start_y + 2, anchor), (NRHS, 2, 2, CY, NZ))
        trace_y = lax.dynamic_slice(padded, (anchor, anchor, start_x + 2, start_y, anchor), (NRHS, 2, CX, 2, NZ))
        source_term = lax.dynamic_slice(forcing, (anchor, anchor, start_x, start_y, anchor), (NRHS, 2, CX, CY, NZ))
        local_slowness = lax.dynamic_slice(slowness, (start_x, start_y, anchor), (CX, CY, NZ))
        solved = tile_solve(source_term, trace_x, trace_y, local_slowness, tables)
        return lax.dynamic_update_slice(wavefield, solved, (anchor, anchor, start_x, start_y, anchor))
    wavefield = lax.fori_loop(0, N_GX * N_GY, visit, jnp.zeros_like(forcing))
    padded = jnp.pad(wavefield, ((0, 0), (0, 0), (2, 2), (2, 2), (0, 0)))

    def one_source(pair):
        block, force = pair
        return force - apply_operator(block[None], slowness)[0]
    residual = lax.map(one_source, (padded, forcing))
    return (wavefield, residual)
```

```python
import functools

import jax
import jax.numpy as jnp
import numpy as np
from jax import lax
from jax.experimental import pallas as pl
from jax.experimental.pallas import tpu as pltpu
from jax.sharding import PartitionSpec as P

KAPPA = 0.12
DAMPING = 0.3
MESH = pl.DeviceIdType.MESH
F32 = jnp.float32
BF16 = jnp.bfloat16


def split_table(table):
    high = np.asarray(table, np.float32).astype(BF16)
    low = (np.asarray(table, np.float64) - high.astype(np.float64)).astype(np.float32).astype(BF16)
    return high, low


def stacked(table):
    high, low = split_table(table)
    return np.concatenate([high, low, high], axis=1)


def sine_basis(length):
    positions = np.arange(1, length + 1, dtype=np.float64)
    angles = positions * (np.pi / (length + 1))
    return np.sqrt(2.0 / (length + 1)) * np.sin(angles[:, None] * positions[None, :]), angles


def build_tables(size_x, size_y, cells_z):
    sine_x, angle_x = sine_basis(size_x)
    sine_y, angle_y = sine_basis(size_y)
    sine_z, angle_z = sine_basis(cells_z)
    symbol_x = 2.5 - 8.0 / 3.0 * np.cos(angle_x) + np.cos(2.0 * angle_x) / 6.0
    symbol_y = 2.5 - 8.0 / 3.0 * np.cos(angle_y) + np.cos(2.0 * angle_y) / 6.0
    symbol_z = 2.0 - 2.0 * np.cos(angle_z)
    real_part = symbol_x[:, None, None] + symbol_y[None, :, None] + symbol_z - KAPPA
    denominator = real_part * real_part + (KAPPA * DAMPING) ** 2
    inverse_real = (real_part / denominator).reshape(size_x * size_y, cells_z).astype(np.float32)
    inverse_imag = (KAPPA * DAMPING / denominator).reshape(size_x * size_y, cells_z)
    inverse_imag = inverse_imag.astype(np.float32)
    horizontal = stacked(np.kron(sine_x, sine_y))
    high, low = split_table(sine_z)
    vertical = np.concatenate([np.concatenate([high, low], axis=1)] * 2, axis=0)
    eye_x = np.eye(size_x)
    eye_y = np.eye(size_y)

    def inward(sine):
        return (-sine[:, 0] / 12.0, (16.0 * sine[:, 0] - sine[:, 1]) / 12.0)

    spread = [np.kron(v[:, None], eye_y) for v in inward(sine_x)]
    spread += [np.kron(eye_x, v[:, None]) for v in inward(sine_y)]
    gather = [np.kron(sine_x[size_x - 2 + l][None, :], eye_y) for l in range(2)]
    gather += [np.kron(eye_x, sine_y[size_y - 2 + l][None, :]) for l in range(2)]
    edge_x = np.zeros(size_x)
    edge_x[[0, -1]] = 1.0 / 12.0
    edge_y = np.zeros(size_y)
    edge_y[[0, -1]] = 1.0 / 12.0
    edges = np.repeat((edge_x[:, None] + edge_y[None, :]).reshape(-1, 1), cells_z, axis=1)
    return (
        horizontal,
        vertical,
        stacked(np.concatenate(spread, axis=1)),
        stacked(np.concatenate(gather, axis=0)),
        inverse_real,
        inverse_imag,
        edges.astype(np.float32),
    )


def split(values):
    high = values.astype(BF16)
    return high, (values - high.astype(F32)).astype(BF16)


def product(table, values):
    high, low = split(values)
    return jnp.dot(
        table, jnp.concatenate([high, high, low], axis=0), preferred_element_type=F32
    )


def along_z(values, vertical):
    half = values.shape[1] // 2
    high, low = split(values)
    outs = []
    for part in range(2):
        lanes = slice(part * half, (part + 1) * half)
        both = jnp.concatenate([high[:, lanes], low[:, lanes]], axis=1)
        mixed = jnp.dot(both, vertical, preferred_element_type=F32)
        outs.append(mixed[:, :half] + mixed[:, half:])
    return jnp.concatenate(outs, axis=1)


def times(real, imag, values):
    half = values.shape[1] // 2
    first, second = values[:, :half], values[:, half:]
    return jnp.concatenate(
        [real * first - imag * second, real * second + imag * first], axis=1
    )


def kernel(
    grid_rows, grid_cols, cells,
    rs_ref, slow_ref, cells_ref, amp_ref,
    hor_ref, ver_ref, spread_ref, gather_ref, lam_r, lam_i, edge_ref,
    wave_ref, resid_ref,
    fhat, spec, inner, inbound, outbound, back_x, back_y, after_x, after_y,
    send_sem, recv_sem, back_send, back_recv,
):
    size_x, size_y, size_z = cells
    rows = size_x * size_y
    count = rs_ref.shape[0]
    row = lax.axis_index("gx")
    col = lax.axis_index("gy")
    has_prev = (row > 0, col > 0)
    has_next = (row < grid_rows - 1, col < grid_cols - 1)
    nexts = ({"gx": row + 1}, {"gy": col + 1})
    prevs = ({"gx": row - 1}, {"gy": col - 1})
    barrier = pltpu.get_barrier_semaphore()
    for axis in range(2):
        @pl.when(has_prev[axis])
        def _():
            pl.semaphore_signal(barrier, inc=1, device_id=prevs[axis], device_id_type=MESH)

        @pl.when(has_next[axis])
        def _():
            pl.semaphore_signal(barrier, inc=1, device_id=nexts[axis], device_id_type=MESH)

    def forward(values):
        return product(hor_ref[...], along_z(values, ver_ref[...]))

    def medium():
        contrast = slow_ref[...] - 1.0
        return KAPPA * contrast - edge_ref[...], (KAPPA * DAMPING) * contrast

    def modes(values):
        return times(lam_r[...], lam_i[...], values)

    row_ids = lax.broadcasted_iota(jnp.int32, (rows, size_z), 0)
    lane_ids = lax.broadcasted_iota(jnp.int32, (rows, size_z), 1)
    cell_x = row_ids // size_y + row * size_x
    cell_y = row_ids % size_y + col * size_y
    flat = (cell_x * (size_y * grid_cols) + cell_y) * size_z + lane_ids

    def forcing(s):
        real = rs_ref[s, 0]
        imag = rs_ref[s, 1]
        for p in range(cells_ref.shape[1]):
            hit = flat == cells_ref[s, p]
            real = real + jnp.where(hit, amp_ref[s, 2 * p], 0.0)
            imag = imag + jnp.where(hit, amp_ref[s, 2 * p + 1], 0.0)
        return jnp.concatenate([real, imag], axis=1)

    def prepare(s, _):
        fhat[s] = forward(forcing(s))
        return 0

    lax.fori_loop(0, count, prepare, 0)
    for axis in range(2):
        @pl.when(jnp.logical_not(has_prev[axis]))
        def _():
            inbound[:, axis] = jnp.zeros_like(inbound[:, axis])

    peers = sum(flag.astype(jnp.int32) for flag in has_prev + has_next)
    pl.semaphore_wait(barrier, peers)

    def onward(s, axis):
        return pltpu.make_async_remote_copy(
            src_ref=outbound.at[s, axis],
            dst_ref=inbound.at[s, axis],
            send_sem=send_sem.at[s, axis],
            recv_sem=recv_sem.at[s, axis],
            device_id=nexts[axis],
            device_id_type=MESH,
        )

    def backward(s, axis):
        source, target = ((back_x, after_x), (back_y, after_y))[axis]
        return pltpu.make_async_remote_copy(
            src_ref=source.at[s],
            dst_ref=target.at[s],
            send_sem=back_send.at[s, axis],
            recv_sem=back_recv.at[s, axis],
            device_id=prevs[axis],
            device_id_type=MESH,
        )

    def chain(s, _):
        for axis in range(2):
            @pl.when(has_prev[axis])
            def _():
                onward(s, axis).wait_recv()
        traces = jnp.concatenate([inbound[s, 0], inbound[s, 1]], axis=0)
        ghat = fhat[s] + product(spread_ref[...], traces)
        fhat[s] = ghat
        spec[s] = modes(ghat)
        for sweep in range(2):
            real, imag = medium()
            physical = times(real, imag, forward(spec[s]))
            inner[s] = physical
            spec[s] = modes(fhat[s] + forward(physical))
        out = product(gather_ref[...], spec[s])
        half = 2 * size_y
        outbound[s, 0] = out[:half]
        outbound[s, 1] = out[half:]
        for axis in range(2):
            @pl.when(has_next[axis])
            def _():
                onward(s, axis).start()
        return 0

    lax.fori_loop(0, count, chain, 0)

    def finish(s, _):
        wave = forward(spec[s])
        spec[s] = wave
        back_x[s] = wave[: 2 * size_y]
        real, imag = medium()
        inner[s] = times(real, imag, wave) - inner[s]
        wave_ref[s, 0] = wave[:, :size_z]
        wave_ref[s, 1] = wave[:, size_z:]
        for l in range(2):
            for c in range(2):
                back_y[s, l, :, c * size_z : (c + 1) * size_z] = wave_ref[
                    s, c, pl.ds(l, size_x, stride=size_y), :
                ]
        for axis in range(2):
            @pl.when(has_prev[axis])
            def _():
                backward(s, axis).start()
        return 0

    lax.fori_loop(0, count, finish, 0)

    def close(s, _):
        for c in range(2):
            resid_ref[s, c] = inner[s, :, c * size_z : (c + 1) * size_z]

        @pl.when(has_next[0])
        def _():
            backward(s, 0).wait_recv()
            near = after_x[s, :size_y]
            far = after_x[s, size_y:]
            for c in range(2):
                lanes = slice(c * size_z, (c + 1) * size_z)
                resid_ref[s, c, rows - 2 * size_y : rows - size_y] -= near[:, lanes] / 12.0
                resid_ref[s, c, rows - size_y :] += (16.0 * near - far)[:, lanes] / 12.0

        @pl.when(has_next[1])
        def _():
            backward(s, 1).wait_recv()
            near = after_y[s, 0]
            far = after_y[s, 1]
            for c in range(2):
                lanes = slice(c * size_z, (c + 1) * size_z)
                below = pl.ds(size_y - 2, size_x, stride=size_y)
                last = pl.ds(size_y - 1, size_x, stride=size_y)
                resid_ref[s, c, below, :] = resid_ref[s, c, below, :] - near[:, lanes] / 12.0
                resid_ref[s, c, last, :] = (
                    resid_ref[s, c, last, :] + (16.0 * near - far)[:, lanes] / 12.0
                )
        for axis in range(2):
            @pl.when(has_next[axis])
            def _():
                onward(s, axis).wait_send()

            @pl.when(has_prev[axis])
            def _():
                backward(s, axis).wait_send()
        return 0

    lax.fori_loop(0, count, close, 0)


def solution(mesh):
    grid_rows, grid_cols = mesh.shape["gx"], mesh.shape["gy"]

    def body(right_side, slowness, source_cells, source_amplitudes):
        count, parts, size_x, size_y, size_z = right_side.shape
        rows = size_x * size_y
        wide = 2 * size_z
        tables = build_tables(size_x, size_y, size_z)
        full = pl.BlockSpec(memory_space=pltpu.VMEM)
        scalars = pl.BlockSpec(memory_space=pltpu.SMEM)
        block = jax.ShapeDtypeStruct((count, parts, rows, size_z), F32)
        wave, resid = pl.pallas_call(
            functools.partial(kernel, grid_rows, grid_cols, (size_x, size_y, size_z)),
            out_shape=(block, block),
            in_specs=[full, full, scalars, scalars] + [full] * len(tables),
            out_specs=(full, full),
            scratch_shapes=[
                pltpu.VMEM((count, rows, wide), F32),
                pltpu.VMEM((count, rows, wide), F32),
                pltpu.VMEM((count, rows, wide), F32),
                pltpu.VMEM((count, 2, 2 * size_y, wide), F32),
                pltpu.VMEM((count, 2, 2 * size_y, wide), F32),
                pltpu.VMEM((count, 2 * size_y, wide), F32),
                pltpu.VMEM((count, 2, size_x, wide), F32),
                pltpu.VMEM((count, 2 * size_y, wide), F32),
                pltpu.VMEM((count, 2, size_x, wide), F32),
                pltpu.SemaphoreType.DMA((count, 2)),
                pltpu.SemaphoreType.DMA((count, 2)),
                pltpu.SemaphoreType.DMA((count, 2)),
                pltpu.SemaphoreType.DMA((count, 2)),
            ],
            compiler_params=pltpu.CompilerParams(collective_id=0, has_side_effects=True),
        )(
            right_side.reshape(count, parts, rows, size_z),
            slowness.reshape(rows, size_z),
            source_cells,
            source_amplitudes.reshape(count, -1),
            *[jnp.asarray(t) for t in tables],
        )
        shape = (count, parts, size_x, size_y, size_z)
        return (wave.reshape(shape), resid.reshape(shape))

    return jax.shard_map(
        body,
        mesh=mesh,
        in_specs=(P(None, None, "gx", "gy", None), P("gx", "gy", None), P(), P()),
        out_specs=(P(None, None, "gx", "gy", None), P(None, None, "gx", "gy", None)),
        check_vma=False,
    )
```

```python
import functools

import jax
import jax.numpy as jnp
import numpy as np
from jax import lax
from jax.experimental import pallas as pl
from jax.experimental.pallas import tpu as pltpu
from jax.sharding import PartitionSpec as P

KAPPA = 0.12
DAMPING = 0.3
MESH = pl.DeviceIdType.MESH
F32 = jnp.float32
BF16 = jnp.bfloat16


def split_table(table):
    high = np.asarray(table, np.float32).astype(BF16)
    low = (np.asarray(table, np.float64) - high.astype(np.float64)).astype(np.float32).astype(BF16)
    return high, low


def stacked(table):
    high, low = split_table(table)
    return np.concatenate([high, low, high], axis=1)


def sine_basis(length):
    positions = np.arange(1, length + 1, dtype=np.float64)
    angles = positions * (np.pi / (length + 1))
    return np.sqrt(2.0 / (length + 1)) * np.sin(angles[:, None] * positions[None, :]), angles


def build_tables(size_x, size_y, cells_z):
    sine_x, angle_x = sine_basis(size_x)
    sine_y, angle_y = sine_basis(size_y)
    sine_z, angle_z = sine_basis(cells_z)
    symbol_x = 2.5 - 8.0 / 3.0 * np.cos(angle_x) + np.cos(2.0 * angle_x) / 6.0
    symbol_y = 2.5 - 8.0 / 3.0 * np.cos(angle_y) + np.cos(2.0 * angle_y) / 6.0
    symbol_z = 2.0 - 2.0 * np.cos(angle_z)
    real_part = symbol_x[:, None, None] + symbol_y[None, :, None] + symbol_z - KAPPA
    denominator = real_part * real_part + (KAPPA * DAMPING) ** 2
    inverse_real = (real_part / denominator).reshape(size_x * size_y, cells_z).astype(np.float32)
    inverse_imag = (KAPPA * DAMPING / denominator).reshape(size_x * size_y, cells_z)
    inverse_imag = inverse_imag.astype(np.float32)
    half_x, half_y = size_x // 2, size_y // 2
    order = np.arange(size_x * size_y).reshape(half_x, 2, half_y, 2)
    order = order.transpose(1, 3, 0, 2).reshape(-1)
    folded = np.arange(size_x * size_y).reshape(size_x, 2, half_y)
    folded[:, 1] = folded[:, 1, ::-1]
    folded = folded.reshape(-1)
    blocks = [
        np.kron(sine_x[:half_x, a::2], sine_y[:half_y, b::2]) for a in range(2) for b in range(2)
    ]
    outward = np.stack([stacked(block) for block in blocks])
    inverse = np.stack([stacked(block.T) for block in blocks])
    horizontal = stacked(np.kron(sine_x, sine_y)[order])
    high, low = split_table(sine_z)
    vertical = np.concatenate([np.concatenate([high, low], axis=1)] * 2, axis=0)
    eye_x = np.eye(size_x)
    eye_y = np.eye(size_y)

    def inward(sine):
        return (-sine[:, 0] / 12.0, (16.0 * sine[:, 0] - sine[:, 1]) / 12.0)

    spread = [np.kron(v[:, None], eye_y) for v in inward(sine_x)]
    spread += [np.kron(eye_x, v[:, None]) for v in inward(sine_y)]
    gather = [np.kron(sine_x[size_x - 2 + l][None, :], eye_y) for l in range(2)]
    gather += [np.kron(eye_x, sine_y[size_y - 2 + l][None, :]) for l in range(2)]
    edge_x = np.zeros(size_x)
    edge_x[[0, -1]] = 1.0 / 12.0
    edge_y = np.zeros(size_y)
    edge_y[[0, -1]] = 1.0 / 12.0
    edges = np.repeat((edge_x[:, None] + edge_y[None, :]).reshape(-1, 1), cells_z, axis=1)
    return (
        horizontal,
        outward,
        inverse,
        vertical,
        vertical,
        stacked(np.concatenate(spread, axis=1)[order]),
        stacked(np.concatenate(gather, axis=0)[:, order]),
        inverse_real[order],
        inverse_imag[order],
        edges[folded].astype(np.float32),
    )


def split(values):
    high = values.astype(BF16)
    return high, (values - high.astype(F32)).astype(BF16)


def product(table, values):
    high, low = split(values)
    return jnp.dot(
        table, jnp.concatenate([high, high, low], axis=0), preferred_element_type=F32
    )


def by_part(table, values):
    half = values.shape[1] // 2
    return jnp.concatenate(
        [product(table, values[:, p * half : (p + 1) * half]) for p in range(2)], axis=1
    )


def along_z(values, vertical):
    half = values.shape[1] // 2
    outs = []
    for part in range(2):
        high, low = split(values[:, part * half : (part + 1) * half])
        both = jnp.concatenate([high, low], axis=1)
        mixed = jnp.dot(both, vertical[part][...], preferred_element_type=F32)
        outs.append(mixed[:, :half] + mixed[:, half:])
    return jnp.concatenate(outs, axis=1)


def to_physical(values, tables, size_x):
    rows = values.shape[0] // 4
    step = rows * 2 // size_x
    even, odd, even_odd, odd_odd = [
        product(tables[p], values[p * rows : (p + 1) * rows]) for p in range(4)
    ]
    near, far = even + odd, even - odd
    near_odd, far_odd = even_odd + odd_odd, even_odd - odd_odd
    first = (near + near_odd, far + far_odd)
    last = (near - near_odd, far - far_odd)
    slices = [slice(i * step, (i + 1) * step) for i in range(size_x // 2)]
    pieces = [part[at] for at in slices for part in first]
    pieces += [part[at] for at in slices[::-1] for part in last]
    return jnp.concatenate(pieces, axis=0)


def to_modes(values, tables, size_x):
    step = values.shape[0] // (2 * size_x)

    def quadrant(first, half):
        ids = range(size_x // 2) if first else range(size_x - 1, size_x // 2 - 1, -1)
        starts = [(2 * i + half) * step for i in ids]
        return jnp.concatenate([values[at : at + step] for at in starts], axis=0)

    top = (quadrant(True, 0), quadrant(True, 1))
    bottom = (quadrant(False, 0), quadrant(False, 1))
    even = [t + b for t, b in zip(top, bottom)]
    odd = [t - b for t, b in zip(top, bottom)]
    folded = [even[0] + even[1], even[0] - even[1], odd[0] + odd[1], odd[0] - odd[1]]
    return jnp.concatenate([product(tables[p], folded[p]) for p in range(4)], axis=0)


def times(real, imag, values):
    half = values.shape[1] // 2
    first, second = values[:, :half], values[:, half:]
    return jnp.concatenate(
        [real * first - imag * second, real * second + imag * first], axis=1
    )


def kernel(
    grid_rows, grid_cols, cells, group,
    rs_ref, slow_ref, cells_ref, amp_ref,
    hor_ref, outw_ref, inv_ref, ver_ref, ver2_ref, spread_ref, gather_ref, lam_r, lam_i, edge_ref,
    wave_ref, resid_ref,
    fhat, spec, inner, contrast, free_out, inbound, back_x, back_y, after_x, after_y,
    medium_in, free_in, x_line, y_line, y_out, bound_hat, bound_spec,
    medium_send, medium_recv, free_send, free_recv, home_send, home_recv,
    x_send, x_recv, y_send, y_recv, back_send, back_recv,
):
    size_x, size_y, size_z = cells
    rows = size_x * size_y
    count = rs_ref.shape[0]
    row = lax.axis_index("gx")
    col = lax.axis_index("gy")
    place = row % group
    first_row = row - place
    odd = col % 2
    solves = jnp.logical_and(odd == 0, place < 4)
    own_rhs = place // 2
    own_col = col + row % 2

    def device(gx, gy):
        return {"gx": gx, "gy": gy}

    def same(gx, gy):
        return jnp.logical_and(gx == row, gy == col)

    def other(gx, gy):
        return jnp.logical_not(same(gx, gy))

    def solver(s):
        return first_row + 2 * s + odd, col - odd

    def home(k):
        return first_row + k, own_col

    has_prev = (row > 0, col > 0)
    has_next = (row < grid_rows - 1, col < grid_cols - 1)
    nexts = ((row + 1, col), (row, col + 1))
    prevs = ((row - 1, col), (row, col - 1))
    turn = row % 2
    line_prev = (row - group, col), (row + 1 - 2 * turn, col - 2 + 2 * turn)
    line_next = (row + group, col), (row + 1 - 2 * turn, col + 2 * turn)
    line_has_prev = (first_row > 0, own_col > 0)
    line_has_next = (first_row + group < grid_rows, own_col < grid_cols - 1)

    barrier = pltpu.get_barrier_semaphore()

    def greet(flag, target):
        @pl.when(flag)
        def _():
            pl.semaphore_signal(
                barrier, inc=1, device_id=device(*target), device_id_type=MESH
            )

    def number(flag):
        return flag.astype(jnp.int32)

    for s in range(count):
        greet(other(*solver(s)), solver(s))
    for axis in range(2):
        greet(has_next[axis], nexts[axis])

    @pl.when(solves)
    def _():
        for k in range(group):
            greet(other(*home(k)), home(k))
        for axis in range(2):
            greet(line_has_prev[axis], line_prev[axis])

    def copy(source, target, sent, received, peer):
        return pltpu.make_async_remote_copy(
            src_ref=source,
            dst_ref=target,
            send_sem=sent,
            recv_sem=received,
            device_id=device(*peer),
            device_id_type=MESH,
        )

    def give_medium(s):
        return copy(
            contrast, medium_in.at[place], medium_send.at[s], medium_recv.at[place], solver(s)
        )

    def give_free(s):
        return copy(
            free_out.at[s], free_in.at[place], free_send.at[s], free_recv.at[place], solver(s)
        )

    def take_medium(k):
        return copy(
            contrast, medium_in.at[k], medium_send.at[0], medium_recv.at[k], home(k)
        )

    def take_free(k):
        return copy(free_out.at[0], free_in.at[k], free_send.at[0], free_recv.at[k], home(k))

    def give_home(k, axis):
        line = (x_line, y_line)[axis]
        return copy(
            line.at[k],
            inbound.at[own_rhs, axis],
            home_send.at[k, axis],
            home_recv.at[own_rhs, axis],
            home(k),
        )

    def take_home(s, axis):
        line = (x_line, y_line)[axis]
        return copy(
            line.at[0], inbound.at[s, axis], home_send.at[0, axis], home_recv.at[s, axis],
            solver(s),
        )

    pass_x = copy(x_line.at[group], x_line.at[0], x_send, x_recv, line_next[0])

    def pass_y(k):
        return copy(y_out.at[k], y_line.at[k], y_send.at[k], y_recv.at[k], line_next[1])

    def backward(s, axis):
        source, target = ((back_x, after_x), (back_y, after_y))[axis]
        return copy(
            source.at[s], target.at[s], back_send.at[s, axis], back_recv.at[s, axis], prevs[axis]
        )

    vertical = (ver_ref, ver2_ref)

    def physical_of(values):
        return to_physical(along_z(values, vertical), outw_ref, size_x)

    def modes_of(values):
        return to_modes(along_z(values, vertical), inv_ref, size_x)

    def modes(values):
        return times(lam_r[...], lam_i[...], values)

    def load(ref):
        return jnp.concatenate([ref[0], ref[1]], axis=1)

    def save(ref, values):
        ref[0] = values[:, :size_z]
        ref[1] = values[:, size_z:]

    def through(medium, values):
        scaled = medium[...]
        return times(scaled - edge_ref[...], DAMPING * scaled, values)

    def sweeps(hat, work, medium, keep=None):
        save(work, modes(load(hat)))
        for sweep in range(2):
            physical = through(medium, physical_of(load(work)))
            if keep is not None:
                save(keep, physical)
            save(work, modes(load(hat) + modes_of(physical)))

    def traces_of(work):
        return by_part(gather_ref[...], load(work))

    def spread_of(first, second):
        return by_part(spread_ref[...], jnp.concatenate([first, second], axis=0))

    half = 2 * size_y
    upper = size_y // 2
    for t in range(upper):
        contrast[pl.ds(t, size_x, stride=size_y), :] = KAPPA * (
            slow_ref[pl.ds(t, size_x, stride=size_y), :] - 1.0
        )
        contrast[pl.ds(upper + t, size_x, stride=size_y), :] = KAPPA * (
            slow_ref[pl.ds(size_y - 1 - t, size_x, stride=size_y), :] - 1.0
        )

    row_ids = lax.broadcasted_iota(jnp.int32, (rows, size_z), 0)
    lane_ids = lax.broadcasted_iota(jnp.int32, (rows, size_z), 1)
    cell_x = row_ids // size_y + row * size_x
    cell_y = row_ids % size_y + col * size_y
    flat = (cell_x * (size_y * grid_cols) + cell_y) * size_z + lane_ids

    def forcing(s):
        real = rs_ref[s, 0]
        imag = rs_ref[s, 1]
        for p in range(cells_ref.shape[1]):
            hit = flat == cells_ref[s, p]
            real = real + jnp.where(hit, amp_ref[s, 0, p], 0.0)
            imag = imag + jnp.where(hit, amp_ref[s, 1, p], 0.0)
        return jnp.concatenate([real, imag], axis=1)

    peers = sum(number(other(*solver(s))) for s in range(count))
    peers = peers + sum(number(flag) for flag in has_prev)
    line_peers = sum(number(other(*home(k))) for k in range(group))
    line_peers = line_peers + sum(number(flag) for flag in line_has_next)
    pl.semaphore_wait(barrier, peers + jnp.where(solves, line_peers, 0))

    def if_other(flag_target, action):
        @pl.when(other(*flag_target))
        def _():
            action()

    for s in range(count):
        if_other(solver(s), give_medium(s).start)

    @pl.when(solves)
    def _():
        @pl.when(first_row == 0)
        def _():
            x_line[0] = jnp.zeros_like(x_line[0])

        @pl.when(own_col == 0)
        def _():
            y_line[...] = jnp.zeros_like(y_line)

    def prepare(step, _):
        s = count - 1 - step
        hat = product(hor_ref[...], along_z(forcing(s), vertical))
        save(fhat.at[s], hat)
        sweeps(fhat.at[s], spec.at[s], contrast)
        out = traces_of(spec.at[s])
        free_out[s, 0] = out[:half]
        free_out[s, 1] = out[half:]
        if_other(solver(s), give_free(s).start)
        return 0

    lax.fori_loop(0, count, prepare, 0)

    def advance(k, _):
        tile_row, tile_col = home(k)
        mine = same(tile_row, tile_col)

        @pl.when(mine)
        def _():
            medium_in[k] = contrast[...]
            free_in[k] = free_out[own_rhs]

        @pl.when(own_col > 0)
        def _():
            pass_y(k).wait_recv()

        @pl.when(jnp.logical_and(k == 0, first_row > 0))
        def _():
            pass_x.wait_recv()

        @pl.when(mine)
        def _():
            inbound[own_rhs, 0] = x_line[k]
            inbound[own_rhs, 1] = y_line[k]

        @pl.when(jnp.logical_not(mine))
        def _():
            for axis in range(2):
                give_home(k, axis).start()
            take_medium(k).wait_recv()
            take_free(k).wait_recv()

        start = jnp.logical_and(tile_row == 0, tile_col == 0)
        end = jnp.logical_and(tile_row == grid_rows - 1, tile_col == grid_cols - 1)

        @pl.when(start)
        def _():
            x_line[k + 1] = free_in[k, 0]
            y_out[k] = free_in[k, 1]

        @pl.when(jnp.logical_not(jnp.logical_or(start, end)))
        def _():
            save(bound_hat, spread_of(x_line[k], y_line[k]))
            sweeps(bound_hat, bound_spec, medium_in.at[k])
            out = traces_of(bound_spec)
            x_line[k + 1] = free_in[k, 0] + out[:half]
            y_out[k] = free_in[k, 1] + out[half:]

        @pl.when(line_has_next[1])
        def _():
            pass_y(k).start()

        @pl.when(jnp.logical_and(k == group - 1, line_has_next[0]))
        def _():
            pass_x.start()
        return 0

    @pl.when(solves)
    def _():
        lax.fori_loop(0, group, advance, 0)

    def unfold(target, source, s, c):
        for t in range(upper):
            low = pl.ds(t, size_x, stride=size_y)
            target[s, c, low, :] = source[s, c, low, :]
            high = pl.ds(size_y - 1 - t, size_x, stride=size_y)
            target[s, c, high, :] = source[s, c, pl.ds(upper + t, size_x, stride=size_y), :]

    def finish(step, _):
        s = count - 1 - step

        @pl.when(other(*solver(s)))
        def _():
            for axis in range(2):
                take_home(s, axis).wait_recv()

        save(fhat.at[s], load(fhat.at[s]) + spread_of(inbound[s, 0], inbound[s, 1]))
        sweeps(fhat.at[s], spec.at[s], contrast, inner.at[s])
        wave = physical_of(load(spec.at[s]))
        save(inner.at[s], through(contrast, wave) - load(inner.at[s]))
        save(spec.at[s], wave)
        for c in range(2):
            lanes = slice(c * size_z, (c + 1) * size_z)
            unfold(wave_ref, spec, s, c)
            back_x[s, :, lanes] = wave_ref[s, c, :half]
            for l in range(2):
                back_y[s, l, :, lanes] = wave_ref[s, c, pl.ds(l, size_x, stride=size_y), :]
        for axis in range(2):
            @pl.when(has_prev[axis])
            def _():
                backward(s, axis).start()
        return 0

    lax.fori_loop(0, count, finish, 0)

    def close(step, _):
        s = count - 1 - step
        for c in range(2):
            unfold(resid_ref, inner, s, c)

        @pl.when(has_next[0])
        def _():
            backward(s, 0).wait_recv()
            near = after_x[s, :size_y]
            far = after_x[s, size_y:]
            for c in range(2):
                lanes = slice(c * size_z, (c + 1) * size_z)
                resid_ref[s, c, rows - 2 * size_y : rows - size_y] -= near[:, lanes] / 12.0
                resid_ref[s, c, rows - size_y :] += (16.0 * near - far)[:, lanes] / 12.0

        @pl.when(has_next[1])
        def _():
            backward(s, 1).wait_recv()
            near = after_y[s, 0]
            far = after_y[s, 1]
            for c in range(2):
                lanes = slice(c * size_z, (c + 1) * size_z)
                below = pl.ds(size_y - 2, size_x, stride=size_y)
                last = pl.ds(size_y - 1, size_x, stride=size_y)
                resid_ref[s, c, below, :] = resid_ref[s, c, below, :] - near[:, lanes] / 12.0
                resid_ref[s, c, last, :] = (
                    resid_ref[s, c, last, :] + (16.0 * near - far)[:, lanes] / 12.0
                )

        @pl.when(other(*solver(s)))
        def _():
            give_medium(s).wait_send()
            give_free(s).wait_send()

        for axis in range(2):
            @pl.when(has_prev[axis])
            def _():
                backward(s, axis).wait_send()
        return 0

    lax.fori_loop(0, count, close, 0)

    @pl.when(solves)
    def _():
        @pl.when(line_has_next[0])
        def _():
            pass_x.wait_send()

        def settle(k, _):
            @pl.when(other(*home(k)))
            def _():
                for axis in range(2):
                    give_home(k, axis).wait_send()

            @pl.when(line_has_next[1])
            def _():
                pass_y(k).wait_send()
            return 0

        lax.fori_loop(0, group, settle, 0)


def solution(mesh):
    grid_rows, grid_cols = mesh.shape["gx"], mesh.shape["gy"]
    group = 4

    def body(right_side, slowness, source_cells, source_amplitudes):
        count, parts, size_x, size_y, size_z = right_side.shape
        rows = size_x * size_y
        wide = 2 * size_z
        tables = build_tables(size_x, size_y, size_z)
        dma = pltpu.SemaphoreType.DMA

        def field(*lead):
            return pltpu.VMEM((*lead, 2, rows, size_z), F32)

        def traces(*lead):
            return pltpu.VMEM((*lead, 2 * size_y, wide), F32)

        full = pl.BlockSpec(memory_space=pltpu.VMEM)
        scalars = pl.BlockSpec(memory_space=pltpu.SMEM)
        block = jax.ShapeDtypeStruct((count, parts, rows, size_z), F32)
        wave, resid = pl.pallas_call(
            functools.partial(kernel, grid_rows, grid_cols, (size_x, size_y, size_z), group),
            out_shape=(block, block),
            in_specs=[full, full, scalars, scalars] + [full] * len(tables),
            out_specs=(full, full),
            scratch_shapes=[
                field(count),
                field(count),
                field(count),
                pltpu.VMEM((rows, size_z), F32),
                traces(count, 2),
                traces(count, 2),
                traces(count),
                pltpu.VMEM((count, 2, size_x, wide), F32),
                traces(count),
                pltpu.VMEM((count, 2, size_x, wide), F32),
                pltpu.VMEM((group, rows, size_z), F32),
                traces(group, 2),
                traces(group + 1),
                traces(group),
                traces(group),
                field(),
                field(),
                dma((count,)),
                dma((group,)),
                dma((count,)),
                dma((group,)),
                dma((group, 2)),
                dma((count, 2)),
                dma,
                dma,
                dma((group,)),
                dma((group,)),
                dma((count, 2)),
                dma((count, 2)),
            ],
            compiler_params=pltpu.CompilerParams(collective_id=0, has_side_effects=True),
        )(
            right_side.reshape(count, parts, rows, size_z),
            slowness.reshape(rows, size_z),
            source_cells,
            source_amplitudes.transpose(0, 2, 1),
            *[jnp.asarray(t) for t in tables],
        )
        shape = (count, parts, size_x, size_y, size_z)
        return (wave.reshape(shape), resid.reshape(shape))

    return jax.shard_map(
        body,
        mesh=mesh,
        in_specs=(P(None, None, "gx", "gy", None), P("gx", "gy", None), P(), P()),
        out_specs=(P(None, None, "gx", "gy", None), P(None, None, "gx", "gy", None)),
        check_vma=False,
    )
```

```python
import functools

import jax
import jax.numpy as jnp
import numpy as np
from jax import lax
from jax.experimental import pallas as pl
from jax.experimental.pallas import tpu as pltpu
from jax.sharding import PartitionSpec as P

KAPPA = 0.12
DAMPING = 0.3
MESH = pl.DeviceIdType.MESH
F32 = jnp.float32
BF16 = jnp.bfloat16


def split_table(table):
    high = np.asarray(table, np.float32).astype(BF16)
    low = (np.asarray(table, np.float64) - high.astype(np.float64)).astype(np.float32).astype(BF16)
    return high, low


def stacked(table):
    high, low = split_table(table)
    return np.concatenate([high, low, high], axis=1)


def sine_basis(length):
    positions = np.arange(1, length + 1, dtype=np.float64)
    angles = positions * (np.pi / (length + 1))
    return np.sqrt(2.0 / (length + 1)) * np.sin(angles[:, None] * positions[None, :]), angles


def build_tables(size_x, size_y, cells_z):
    sine_x, angle_x = sine_basis(size_x)
    sine_y, angle_y = sine_basis(size_y)
    sine_z, angle_z = sine_basis(cells_z)
    symbol_x = 2.5 - 8.0 / 3.0 * np.cos(angle_x) + np.cos(2.0 * angle_x) / 6.0
    symbol_y = 2.5 - 8.0 / 3.0 * np.cos(angle_y) + np.cos(2.0 * angle_y) / 6.0
    symbol_z = 2.0 - 2.0 * np.cos(angle_z)
    real_part = symbol_x[:, None, None] + symbol_y[None, :, None] + symbol_z - KAPPA
    denominator = real_part * real_part + (KAPPA * DAMPING) ** 2
    inverse_real = (real_part / denominator).reshape(size_x * size_y, cells_z).astype(np.float32)
    inverse_imag = (KAPPA * DAMPING / denominator).reshape(size_x * size_y, cells_z)
    inverse_imag = inverse_imag.astype(np.float32)
    half_x, half_y = size_x // 2, size_y // 2
    order = np.arange(size_x * size_y).reshape(half_x, 2, half_y, 2)
    order = order.transpose(1, 3, 0, 2).reshape(-1)
    folded = np.arange(size_x * size_y).reshape(size_x, 2, half_y)
    folded[:, 1] = folded[:, 1, ::-1]
    folded = folded.reshape(-1)
    blocks = [
        np.kron(sine_x[:half_x, a::2], sine_y[:half_y, b::2]) for a in range(2) for b in range(2)
    ]
    outward = np.stack([stacked(block) for block in blocks])
    inverse = np.stack([stacked(block.T) for block in blocks])
    high, low = split_table(sine_z)
    vertical = np.concatenate([np.concatenate([high, low], axis=1)] * 2, axis=0)
    eye_x = np.eye(size_x)
    eye_y = np.eye(size_y)

    def inward(sine):
        return (-sine[:, 0] / 12.0, (16.0 * sine[:, 0] - sine[:, 1]) / 12.0)

    spread = [np.kron(v[:, None], eye_y) for v in inward(sine_x)]
    spread += [np.kron(eye_x, v[:, None]) for v in inward(sine_y)]
    gather = [np.kron(sine_x[size_x - 2 + l][None, :], eye_y) for l in range(2)]
    gather += [np.kron(eye_x, sine_y[size_y - 2 + l][None, :]) for l in range(2)]
    edge_x = np.zeros(size_x)
    edge_x[[0, -1]] = 1.0 / 12.0
    edge_y = np.zeros(size_y)
    edge_y[[0, -1]] = 1.0 / 12.0
    edges = np.repeat((edge_x[:, None] + edge_y[None, :]).reshape(-1, 1), cells_z, axis=1)
    return (
        outward,
        inverse,
        vertical,
        vertical,
        stacked(np.concatenate(spread, axis=1)[order]),
        stacked(np.concatenate(gather, axis=0)[:, order]),
        inverse_real[order],
        inverse_imag[order],
        edges[folded].astype(np.float32),
    )


def split(values):
    high = values.astype(BF16)
    return high, (values - high.astype(F32)).astype(BF16)


def product(table, values):
    high, low = split(values)
    return jnp.dot(
        table, jnp.concatenate([high, high, low], axis=0), preferred_element_type=F32
    )


def by_part(table, values):
    half = values.shape[1] // 2
    return jnp.concatenate(
        [product(table, values[:, p * half : (p + 1) * half]) for p in range(2)], axis=1
    )


def along_z(values, vertical):
    half = values.shape[1] // 2
    outs = []
    for part in range(2):
        high, low = split(values[:, part * half : (part + 1) * half])
        both = jnp.concatenate([high, low], axis=1)
        mixed = jnp.dot(both, vertical[part][...], preferred_element_type=F32)
        outs.append(mixed[:, :half] + mixed[:, half:])
    return jnp.concatenate(outs, axis=1)


def to_physical(values, tables, size_x):
    rows = values.shape[0] // 4
    step = rows * 2 // size_x
    even, odd, even_odd, odd_odd = [
        product(tables[p], values[p * rows : (p + 1) * rows]) for p in range(4)
    ]
    near, far = even + odd, even - odd
    near_odd, far_odd = even_odd + odd_odd, even_odd - odd_odd
    first = (near + near_odd, far + far_odd)
    last = (near - near_odd, far - far_odd)
    slices = [slice(i * step, (i + 1) * step) for i in range(size_x // 2)]
    pieces = [part[at] for at in slices for part in first]
    pieces += [part[at] for at in slices[::-1] for part in last]
    return jnp.concatenate(pieces, axis=0)


def to_modes(values, tables, size_x):
    step = values.shape[0] // (2 * size_x)

    def quadrant(first, half):
        ids = range(size_x // 2) if first else range(size_x - 1, size_x // 2 - 1, -1)
        starts = [(2 * i + half) * step for i in ids]
        return jnp.concatenate([values[at : at + step] for at in starts], axis=0)

    top = (quadrant(True, 0), quadrant(True, 1))
    bottom = (quadrant(False, 0), quadrant(False, 1))
    even = [t + b for t, b in zip(top, bottom)]
    odd = [t - b for t, b in zip(top, bottom)]
    folded = [even[0] + even[1], even[0] - even[1], odd[0] + odd[1], odd[0] - odd[1]]
    return jnp.concatenate([product(tables[p], folded[p]) for p in range(4)], axis=0)


def times(real, imag, values):
    half = values.shape[1] // 2
    first, second = values[:, :half], values[:, half:]
    return jnp.concatenate(
        [real * first - imag * second, real * second + imag * first], axis=1
    )


def kernel(
    load_inputs, put_wave, put_resid, grid_rows, grid_cols, cells, group,
    rs_ref, slow_ref, cells_ref, amp_ref,
    outw_ref, inv_ref, ver_ref, ver2_ref, spread_ref, gather_ref, lam_r, lam_i, edge_ref,
    wave_ref, resid_ref,
    fhat, spec, inner, contrast, medium, free_out, inbound, back_x, back_y, after_x, after_y,
    medium_in, free_in, x_line, y_line, y_out, bound_hat, bound_spec, line_medium,
    medium_send, medium_recv, free_send, free_recv, home_send, home_recv,
    x_send, x_recv, y_send, y_recv, back_send, back_recv,
):
    size_x, size_y, size_z = cells
    rows = size_x * size_y
    count = rs_ref.shape[0]
    row = lax.axis_index("gx")
    col = lax.axis_index("gy")
    place = row % group
    first_row = row - place
    odd = col % 2
    pair = col // 2
    solves = jnp.logical_and(odd != pair % 2, place < 4)
    own_rhs = place // 2
    own_col = 2 * pair + row % 2

    def device(gx, gy):
        return {"gx": gx, "gy": gy}

    def same(gx, gy):
        return jnp.logical_and(gx == row, gy == col)

    def other(gx, gy):
        return jnp.logical_not(same(gx, gy))

    def solver(s, tile_col=col):
        group_col = tile_col - tile_col % 2
        return first_row + 2 * s + tile_col % 2, group_col + 1 - group_col // 2 % 2

    def home(k):
        return first_row + k, own_col

    def side(k):
        return first_row + k, own_col + 1

    has_prev = (row > 0, col > 0)
    has_next = (row < grid_rows - 1, col < grid_cols - 1)
    nexts = ((row + 1, col), (row, col + 1))
    prevs = ((row - 1, col), (row, col - 1))
    turn = row % 2
    near = pair % 2
    line_prev = (row - group, col), (row + 1 - 2 * turn, col - (1 - turn) * (3 - 2 * near))
    line_next = (row + group, col), (row + 1 - 2 * turn, col + turn * (1 + 2 * near))
    line_has_prev = (first_row > 0, own_col > 0)
    line_has_next = (first_row + group < grid_rows, own_col < grid_cols - 1)

    barrier = pltpu.get_barrier_semaphore()

    def greet(flag, target):
        @pl.when(flag)
        def _():
            pl.semaphore_signal(
                barrier, inc=1, device_id=device(*target), device_id_type=MESH
            )

    def number(flag):
        return flag.astype(jnp.int32)

    before = jnp.maximum(col - 1, 0)
    for s in range(count):
        greet(other(*solver(s)), solver(s))
        greet(jnp.logical_and(col > 0, other(*solver(s, before))), solver(s, before))
    for axis in range(2):
        greet(has_next[axis], nexts[axis])

    @pl.when(solves)
    def _():
        for k in range(group):
            greet(other(*home(k)), home(k))
        for axis in range(2):
            greet(line_has_prev[axis], line_prev[axis])

    load_inputs()

    def copy(source, target, sent, received, peer):
        return pltpu.make_async_remote_copy(
            src_ref=source,
            dst_ref=target,
            send_sem=sent,
            recv_sem=received,
            device_id=device(*peer),
            device_id_type=MESH,
        )

    def give_medium(s):
        return copy(
            contrast, medium_in.at[place], medium_send.at[s], medium_recv.at[place], solver(s)
        )

    def give_free(s):
        return copy(
            free_out.at[s], free_in.at[place], free_send.at[s], free_recv.at[place], solver(s)
        )

    def take_medium(k):
        return copy(
            contrast, medium_in.at[k], medium_send.at[0], medium_recv.at[k], home(k)
        )

    def take_free(k):
        return copy(free_out.at[0], free_in.at[k], free_send.at[0], free_recv.at[k], home(k))

    def give_home(k):
        return copy(
            x_line.at[k],
            inbound.at[own_rhs, 0],
            home_send.at[k, 0],
            home_recv.at[own_rhs, 0],
            home(k),
        )

    def pass_side(k):
        return copy(
            y_out.at[k],
            inbound.at[own_rhs, 1],
            home_send.at[k, 1],
            home_recv.at[own_rhs, 1],
            side(k),
        )

    def take_home(s, axis):
        line = (x_line, y_out)[axis]
        return copy(
            line.at[0], inbound.at[s, axis], home_send.at[0, axis], home_recv.at[s, axis],
            solver(s),
        )

    pass_x = copy(x_line.at[group], x_line.at[0], x_send, x_recv, line_next[0])

    def pass_y(k):
        return copy(y_out.at[k], y_line.at[k], y_send.at[k], y_recv.at[k], line_next[1])

    def backward(s, axis):
        source, target = ((back_x, after_x), (back_y, after_y))[axis]
        return copy(
            source.at[s], target.at[s], back_send.at[s, axis], back_recv.at[s, axis], prevs[axis]
        )

    vertical = (ver_ref, ver2_ref)

    def physical_of(values):
        return to_physical(along_z(values, vertical), outw_ref, size_x)

    def modes_of(values):
        return to_modes(along_z(values, vertical), inv_ref, size_x)

    def modes(values):
        return times(lam_r[...], lam_i[...], values)

    def load(ref):
        return jnp.concatenate([ref[0], ref[1]], axis=1)

    def save(ref, values):
        ref[0] = values[:, :size_z]
        ref[1] = values[:, size_z:]

    def through(factor, values):
        return times(factor[0], factor[1], values)

    def factors(target, scaled):
        target[0] = scaled - edge_ref[...]
        target[1] = DAMPING * scaled

    def sweeps(hat, work, factor, keep=None):
        save(work, modes(load(hat)))
        for sweep in range(2):
            physical = through(factor, physical_of(load(work)))
            if keep is not None:
                save(keep, physical)
            save(work, modes(load(hat) + modes_of(physical)))

    def traces_of(work):
        return by_part(gather_ref[...], load(work))

    def spread_of(first, second):
        return by_part(spread_ref[...], jnp.concatenate([first, second], axis=0))

    half = 2 * size_y
    upper = size_y // 2
    for t in range(upper):
        contrast[pl.ds(t, size_x, stride=size_y), :] = KAPPA * (
            slow_ref[pl.ds(t, size_x, stride=size_y), :] - 1.0
        )
        contrast[pl.ds(upper + t, size_x, stride=size_y), :] = KAPPA * (
            slow_ref[pl.ds(size_y - 1 - t, size_x, stride=size_y), :] - 1.0
        )
    factors(medium, contrast[...])

    points = cells_ref.shape[1]
    row_ids = lax.broadcasted_iota(jnp.int32, (rows, points), 0)
    in_row = row_ids % size_y
    in_row = jnp.where(in_row < upper, in_row, size_y + upper - 1 - in_row)
    row_ids = row_ids - row_ids % size_y + in_row
    lane_ids = lax.broadcasted_iota(jnp.int32, (size_z, points), 0)

    def fold(s):
        for c in range(2):
            for t in range(upper):
                low = pl.ds(t, size_x, stride=size_y)
                inner[s, c, low, :] = rs_ref[s, c, low, :]
                high = pl.ds(size_y - 1 - t, size_x, stride=size_y)
                inner[s, c, pl.ds(upper + t, size_x, stride=size_y), :] = rs_ref[s, c, high, :]

    def forcing(s):
        fold(s)
        flat = cells_ref[pl.ds(s, 1), :]
        at_x = flat // (size_y * grid_cols * size_z) - row * size_x
        at_y = flat // size_z % (size_y * grid_cols) - col * size_y
        inside = jnp.logical_and(
            jnp.logical_and(at_x >= 0, at_x < size_x), jnp.logical_and(at_y >= 0, at_y < size_y)
        )
        at_row = jnp.where(inside, at_x * size_y + at_y, -1)
        where_row = jnp.where(row_ids == at_row, 1.0, 0.0).astype(BF16)
        hit_z = lane_ids == flat % size_z
        outs = []
        for c in range(2):
            rest = jnp.where(hit_z, amp_ref[s, c : c + 1, :], 0.0)
            total = inner[s, c]
            for term in range(3):
                part = rest.astype(BF16)
                rest = rest - part.astype(F32)
                total = total + lax.dot_general(
                    where_row, part, (((1,), (1,)), ((), ())), preferred_element_type=F32
                )
            outs.append(total)
        return jnp.concatenate(outs, axis=1)

    peers = sum(number(other(*solver(s))) for s in range(count))
    peers = peers + sum(number(flag) for flag in has_prev)
    line_peers = sum(number(other(*home(k))) for k in range(group))
    line_peers = line_peers + sum(number(flag) for flag in line_has_next)
    line_peers = line_peers + sum(
        number(jnp.logical_and(line_has_next[1], other(*side(k)))) for k in range(group)
    )

    def if_other(flag_target, action):
        @pl.when(other(*flag_target))
        def _():
            action()

    early = jnp.logical_and(col < grid_cols // 2, jnp.logical_or(place < 2, col == 0))
    corner = jnp.logical_and(row == 0, col == 0)

    @pl.when(col == 0)
    def _():
        inbound[:, 1] = jnp.zeros_like(inbound[:, 1])

    @pl.when(solves)
    def _():
        @pl.when(first_row == 0)
        def _():
            x_line[0] = jnp.zeros_like(x_line[0])

        @pl.when(own_col == 0)
        def _():
            y_line[...] = jnp.zeros_like(y_line)

    def rank(step):
        return jnp.where(place < 2, count - 1 - step, step)

    def open_sends():
        pl.semaphore_wait(barrier, peers + jnp.where(solves, line_peers, 0))
        for s in range(count):
            @pl.when(jnp.logical_and(early, jnp.logical_and(other(*solver(s)), ~corner)))
            def _():
                give_medium(s).start()

        if_other(solver(rank(0)), give_free(rank(0)).start)

    def prepare(step, _):
        s = rank(step)

        @pl.when(step == 1)
        def _():
            open_sends()

        save(fhat.at[s], modes_of(forcing(s)))
        sweeps(fhat.at[s], spec.at[s], medium)
        out = traces_of(spec.at[s])
        free_out[s, 0] = out[:half]
        free_out[s, 1] = out[half:]

        @pl.when(jnp.logical_and(step == 1, other(*solver(s))))
        def _():
            give_free(s).start()
        return 0

    lax.fori_loop(0, count, prepare, 0)
    for s in range(count):
        @pl.when(jnp.logical_and(~early, other(*solver(s))))
        def _():
            give_medium(s).start()

    def advance(k, _):
        tile_row, tile_col = home(k)
        mine = same(tile_row, tile_col)

        start = jnp.logical_and(tile_row == 0, tile_col == 0)
        end = jnp.logical_and(tile_row == grid_rows - 1, tile_col == grid_cols - 1)

        @pl.when(mine)
        def _():
            free_in[k] = free_out[own_rhs]
            line_medium[...] = medium[...]

        @pl.when(jnp.logical_not(jnp.logical_or(mine, start)))
        def _():
            take_medium(k).wait_recv()
            factors(line_medium, medium_in[k])

        @pl.when(jnp.logical_and(k == 0, first_row > 0))
        def _():
            pass_x.wait_recv()

        @pl.when(mine)
        def _():
            inbound[own_rhs, 0] = x_line[k]

        @pl.when(jnp.logical_not(mine))
        def _():
            give_home(k).start()

        @pl.when(own_col > 0)
        def _():
            pass_y(k).wait_recv()

        @pl.when(jnp.logical_not(jnp.logical_or(start, end)))
        def _():
            save(bound_hat, spread_of(x_line[k], y_line[k]))
            sweeps(bound_hat, bound_spec, line_medium)
            out = traces_of(bound_spec)
            x_line[k + 1] = out[:half]
            y_out[k] = out[half:]

        @pl.when(start)
        def _():
            x_line[k + 1] = jnp.zeros_like(x_line[k])
            y_out[k] = jnp.zeros_like(y_out[k])

        @pl.when(jnp.logical_not(mine))
        def _():
            take_free(k).wait_recv()

        @pl.when(jnp.logical_not(end))
        def _():
            x_line[k + 1] += free_in[k, 0]
            y_out[k] += free_in[k, 1]

        @pl.when(jnp.logical_and(k == group - 1, line_has_next[0]))
        def _():
            pass_x.start()

        @pl.when(line_has_next[1])
        def _():
            pass_y(k).start()

            @pl.when(other(*side(k)))
            def _():
                pass_side(k).start()

            @pl.when(same(*side(k)))
            def _():
                inbound[own_rhs, 1] = y_out[k]
        return 0

    @pl.when(solves)
    def _():
        lax.fori_loop(0, group, advance, 0)

    def unfold(target, source, s, c):
        for t in range(upper):
            low = pl.ds(t, size_x, stride=size_y)
            target[s, c, low, :] = source[s, c, low, :]
            high = pl.ds(size_y - 1 - t, size_x, stride=size_y)
            target[s, c, high, :] = source[s, c, pl.ds(upper + t, size_x, stride=size_y), :]

    def finish(step, _):
        s = count - 1 - step

        @pl.when(other(*solver(s)))
        def _():
            take_home(s, 0).wait_recv()

        @pl.when(jnp.logical_and(col > 0, other(*solver(s, before))))
        def _():
            take_home(s, 1).wait_recv()

        save(fhat.at[s], load(fhat.at[s]) + spread_of(inbound[s, 0], inbound[s, 1]))
        sweeps(fhat.at[s], spec.at[s], medium, inner.at[s])
        wave = physical_of(load(spec.at[s]))
        save(inner.at[s], through(medium, wave) - load(inner.at[s]))
        save(spec.at[s], wave)
        for c in range(2):
            lanes = slice(c * size_z, (c + 1) * size_z)
            unfold(wave_ref, spec, s, c)
            back_x[s, :, lanes] = wave_ref[s, c, :half]
            for l in range(2):
                back_y[s, l, :, lanes] = wave_ref[s, c, pl.ds(l, size_x, stride=size_y), :]
        put_wave(s).start()
        for axis in range(2):
            @pl.when(has_prev[axis])
            def _():
                backward(s, axis).start()
        return 0

    lax.fori_loop(0, count, finish, 0)

    def close(step, _):
        s = count - 1 - step
        for c in range(2):
            unfold(resid_ref, inner, s, c)

        @pl.when(has_next[0])
        def _():
            backward(s, 0).wait_recv()
            near = after_x[s, :size_y]
            far = after_x[s, size_y:]
            for c in range(2):
                lanes = slice(c * size_z, (c + 1) * size_z)
                resid_ref[s, c, rows - 2 * size_y : rows - size_y] -= near[:, lanes] / 12.0
                resid_ref[s, c, rows - size_y :] += (16.0 * near - far)[:, lanes] / 12.0

        @pl.when(has_next[1])
        def _():
            backward(s, 1).wait_recv()
            near = after_y[s, 0]
            far = after_y[s, 1]
            for c in range(2):
                lanes = slice(c * size_z, (c + 1) * size_z)
                below = pl.ds(size_y - 2, size_x, stride=size_y)
                last = pl.ds(size_y - 1, size_x, stride=size_y)
                resid_ref[s, c, below, :] = resid_ref[s, c, below, :] - near[:, lanes] / 12.0
                resid_ref[s, c, last, :] = (
                    resid_ref[s, c, last, :] + (16.0 * near - far)[:, lanes] / 12.0
                )

        put_resid(s).start()

        @pl.when(other(*solver(s)))
        def _():
            give_free(s).wait_send()

        @pl.when(jnp.logical_and(other(*solver(s)), ~corner))
        def _():
            give_medium(s).wait_send()

        for axis in range(2):
            @pl.when(has_prev[axis])
            def _():
                backward(s, axis).wait_send()
        return 0

    lax.fori_loop(0, count, close, 0)

    def flush(s, _):
        put_wave(s).wait()
        put_resid(s).wait()
        return 0

    lax.fori_loop(0, count, flush, 0)

    @pl.when(solves)
    def _():
        @pl.when(line_has_next[0])
        def _():
            pass_x.wait_send()

        def settle(k, _):
            @pl.when(other(*home(k)))
            def _():
                give_home(k).wait_send()

            @pl.when(line_has_next[1])
            def _():
                pass_y(k).wait_send()

                @pl.when(other(*side(k)))
                def _():
                    pass_side(k).wait_send()
            return 0

        lax.fori_loop(0, group, settle, 0)


def staged(sizes, inputs, *refs):
    sources, refs = refs[:inputs], refs[inputs:]
    wave_out, resid_out, refs = refs[0], refs[1], refs[2:]
    targets, refs = refs[:inputs], refs[inputs:]
    wave, resid, in_sem, wave_sem, resid_sem, refs = *refs[:5], refs[5:]

    def load_inputs():
        copies = [
            pltpu.make_async_copy(source, target, in_sem.at[i])
            for i, (source, target) in enumerate(zip(sources, targets))
        ]
        for copy in copies:
            copy.start()
        for copy in copies:
            copy.wait()

    def put_wave(s):
        return pltpu.make_async_copy(wave.at[s], wave_out.at[s], wave_sem.at[s])

    def put_resid(s):
        return pltpu.make_async_copy(resid.at[s], resid_out.at[s], resid_sem.at[s])

    kernel(load_inputs, put_wave, put_resid, *sizes, *targets, wave, resid, *refs)


def solution(mesh):
    grid_rows, grid_cols = mesh.shape["gx"], mesh.shape["gy"]
    group = 4

    def body(right_side, slowness, source_cells, source_amplitudes):
        count, parts, size_x, size_y, size_z = right_side.shape
        rows = size_x * size_y
        wide = 2 * size_z
        tables = build_tables(size_x, size_y, size_z)
        dma = pltpu.SemaphoreType.DMA

        def field(*lead):
            return pltpu.VMEM((*lead, 2, rows, size_z), F32)

        def traces(*lead):
            return pltpu.VMEM((*lead, 2 * size_y, wide), F32)

        whole = pl.BlockSpec(memory_space=pl.ANY)
        block = jax.ShapeDtypeStruct((count, parts, rows, size_z), F32)
        operands = (
            right_side.reshape(count, parts, rows, size_z),
            slowness.reshape(rows, size_z),
            source_cells,
            source_amplitudes.transpose(0, 2, 1),
            *[jnp.asarray(t) for t in tables],
        )
        sizes = (grid_rows, grid_cols, (size_x, size_y, size_z), group)
        wave, resid = pl.pallas_call(
            functools.partial(staged, sizes, len(operands)),
            out_shape=(block, block),
            in_specs=[whole] * len(operands),
            out_specs=(whole, whole),
            scratch_shapes=[pltpu.VMEM(o.shape, o.dtype) for o in operands]
            + [pltpu.VMEM(block.shape, F32)] * 2
            + [dma((len(operands),)), dma((count,)), dma((count,))]
            + [
                field(count),
                field(count),
                field(count),
                pltpu.VMEM((rows, size_z), F32),
                field(),
                traces(count, 2),
                traces(count, 2),
                traces(count),
                pltpu.VMEM((count, 2, size_x, wide), F32),
                traces(count),
                pltpu.VMEM((count, 2, size_x, wide), F32),
                pltpu.VMEM((group, rows, size_z), F32),
                traces(group, 2),
                traces(group + 1),
                traces(group),
                traces(group),
                field(),
                field(),
                field(),
                dma((count,)),
                dma((group,)),
                dma((count,)),
                dma((group,)),
                dma((group, 2)),
                dma((count, 2)),
                dma,
                dma,
                dma((group,)),
                dma((group,)),
                dma((count, 2)),
                dma((count, 2)),
            ],
            compiler_params=pltpu.CompilerParams(collective_id=0, has_side_effects=True),
        )(*operands)
        shape = (count, parts, size_x, size_y, size_z)
        return (wave.reshape(shape), resid.reshape(shape))

    return jax.shard_map(
        body,
        mesh=mesh,
        in_specs=(P(None, None, "gx", "gy", None), P("gx", "gy", None), P(), P()),
        out_specs=(P(None, None, "gx", "gy", None), P(None, None, "gx", "gy", None)),
        check_vma=False,
    )
```

```python
import functools

import jax
import jax.numpy as jnp
import numpy as np
from jax import lax
from jax.experimental import pallas as pl
from jax.experimental.pallas import tpu as pltpu
from jax.sharding import PartitionSpec as P

KAPPA = 0.12
DAMPING = 0.3
MESH = pl.DeviceIdType.MESH
F32 = jnp.float32
BF16 = jnp.bfloat16


def split_table(table):
    high = np.asarray(table, np.float32).astype(BF16)
    low = (np.asarray(table, np.float64) - high.astype(np.float64)).astype(np.float32).astype(BF16)
    return high, low


def stacked(table):
    high, low = split_table(table)
    return np.concatenate([high, low, high], axis=1)


def sine_basis(length):
    positions = np.arange(1, length + 1, dtype=np.float64)
    angles = positions * (np.pi / (length + 1))
    return np.sqrt(2.0 / (length + 1)) * np.sin(angles[:, None] * positions[None, :]), angles


def build_tables(size_x, size_y, cells_z):
    sine_x, angle_x = sine_basis(size_x)
    sine_y, angle_y = sine_basis(size_y)
    sine_z, angle_z = sine_basis(cells_z)
    symbol_x = 2.5 - 8.0 / 3.0 * np.cos(angle_x) + np.cos(2.0 * angle_x) / 6.0
    symbol_y = 2.5 - 8.0 / 3.0 * np.cos(angle_y) + np.cos(2.0 * angle_y) / 6.0
    symbol_z = 2.0 - 2.0 * np.cos(angle_z)
    real_part = symbol_x[:, None, None] + symbol_y[None, :, None] + symbol_z - KAPPA
    denominator = real_part * real_part + (KAPPA * DAMPING) ** 2
    inverse_real = (real_part / denominator).reshape(size_x * size_y, cells_z).astype(np.float32)
    inverse_imag = (KAPPA * DAMPING / denominator).reshape(size_x * size_y, cells_z)
    inverse_imag = inverse_imag.astype(np.float32)
    half_x, half_y = size_x // 2, size_y // 2
    order = np.arange(size_x * size_y).reshape(half_x, 2, half_y, 2)
    order = order.transpose(1, 3, 0, 2).reshape(-1)
    folded = np.arange(size_x * size_y).reshape(size_x, 2, half_y)
    folded[:, 1] = folded[:, 1, ::-1]
    folded = folded.reshape(-1)
    blocks = [
        np.kron(sine_x[:half_x, a::2], sine_y[:half_y, b::2]) for a in range(2) for b in range(2)
    ]
    outward = np.stack([stacked(block) for block in blocks])
    inverse = np.stack([stacked(block.T) for block in blocks])
    high, low = split_table(sine_z)
    vertical = np.concatenate([np.concatenate([high, low], axis=1)] * 2, axis=0)
    eye_x = np.eye(size_x)
    eye_y = np.eye(size_y)

    def inward(sine):
        return (-sine[:, 0] / 12.0, (16.0 * sine[:, 0] - sine[:, 1]) / 12.0)

    spread = [np.kron(v[:, None], eye_y) for v in inward(sine_x)]
    spread += [np.kron(eye_x, v[:, None]) for v in inward(sine_y)]
    gather = [np.kron(sine_x[size_x - 2 + l][None, :], eye_y) for l in range(2)]
    gather += [np.kron(eye_x, sine_y[size_y - 2 + l][None, :]) for l in range(2)]
    edge_x = np.zeros(size_x)
    edge_x[[0, -1]] = 1.0 / 12.0
    edge_y = np.zeros(size_y)
    edge_y[[0, -1]] = 1.0 / 12.0
    edges = np.repeat((edge_x[:, None] + edge_y[None, :]).reshape(-1, 1), cells_z, axis=1)
    return (
        outward,
        inverse,
        vertical,
        vertical,
        stacked(np.concatenate(spread, axis=1)[order]),
        stacked(np.concatenate(gather, axis=0)[:, order]),
        inverse_real[order],
        inverse_imag[order],
        edges[folded].astype(np.float32),
    )


def split(values):
    high = values.astype(BF16)
    return high, (values - high.astype(F32)).astype(BF16)


def product(table, values):
    high, low = split(values)
    return jnp.dot(
        table, jnp.concatenate([high, high, low], axis=0), preferred_element_type=F32
    )


def by_part(table, values):
    half = values.shape[1] // 2
    return jnp.concatenate(
        [product(table, values[:, p * half : (p + 1) * half]) for p in range(2)], axis=1
    )


def along_z(values, vertical):
    half = values.shape[1] // 2
    outs = []
    for part in range(2):
        high, low = split(values[:, part * half : (part + 1) * half])
        both = jnp.concatenate([high, low], axis=1)
        mixed = jnp.dot(both, vertical[part][...], preferred_element_type=F32)
        outs.append(mixed[:, :half] + mixed[:, half:])
    return jnp.concatenate(outs, axis=1)


def to_physical(values, tables, size_x):
    rows = values.shape[0] // 4
    step = rows * 2 // size_x
    even, odd, even_odd, odd_odd = [
        product(tables[p], values[p * rows : (p + 1) * rows]) for p in range(4)
    ]
    near, far = even + odd, even - odd
    near_odd, far_odd = even_odd + odd_odd, even_odd - odd_odd
    first = (near + near_odd, far + far_odd)
    last = (near - near_odd, far - far_odd)
    slices = [slice(i * step, (i + 1) * step) for i in range(size_x // 2)]
    pieces = [part[at] for at in slices for part in first]
    pieces += [part[at] for at in slices[::-1] for part in last]
    return jnp.concatenate(pieces, axis=0)


def to_modes(values, tables, size_x):
    step = values.shape[0] // (2 * size_x)

    def quadrant(first, half):
        ids = range(size_x // 2) if first else range(size_x - 1, size_x // 2 - 1, -1)
        starts = [(2 * i + half) * step for i in ids]
        return jnp.concatenate([values[at : at + step] for at in starts], axis=0)

    top = (quadrant(True, 0), quadrant(True, 1))
    bottom = (quadrant(False, 0), quadrant(False, 1))
    even = [t + b for t, b in zip(top, bottom)]
    odd = [t - b for t, b in zip(top, bottom)]
    folded = [even[0] + even[1], even[0] - even[1], odd[0] + odd[1], odd[0] - odd[1]]
    return jnp.concatenate([product(tables[p], folded[p]) for p in range(4)], axis=0)


def times(real, imag, values):
    half = values.shape[1] // 2
    first, second = values[:, :half], values[:, half:]
    return jnp.concatenate(
        [real * first - imag * second, real * second + imag * first], axis=1
    )


def kernel(
    load_inputs, grid_rows, grid_cols, cells, group,
    rs_ref, slow_ref, cells_ref, amp_ref,
    outw_ref, inv_ref, ver_ref, ver2_ref, spread_ref, gather_ref, lam_r, lam_i, edge_ref,
    wave_ref, resid_ref,
    fhat, spec, inner, contrast, medium, free_out, inbound, back_x, back_y, after_x, after_y,
    medium_in, free_in, x_line, y_line, y_out, bound_hat, bound_spec, line_medium,
    medium_send, medium_recv, free_send, free_recv, home_send, home_recv,
    x_send, x_recv, y_send, y_recv, back_send, back_recv,
):
    size_x, size_y, size_z = cells
    rows = size_x * size_y
    count = rs_ref.shape[0]
    row = lax.axis_index("gx")
    col = lax.axis_index("gy")
    place = row % group
    first_row = row - place
    odd = col % 2
    pair = col // 2
    solves = jnp.logical_and(odd != pair % 2, place < 4)
    own_rhs = place // 2
    own_col = 2 * pair + row % 2

    def device(gx, gy):
        return {"gx": gx, "gy": gy}

    def same(gx, gy):
        return jnp.logical_and(gx == row, gy == col)

    def other(gx, gy):
        return jnp.logical_not(same(gx, gy))

    def solver(s, tile_col=col):
        group_col = tile_col - tile_col % 2
        return first_row + 2 * s + tile_col % 2, group_col + 1 - group_col // 2 % 2

    def home(k):
        return first_row + k, own_col

    def side(k):
        return first_row + k, own_col + 1

    has_prev = (row > 0, col > 0)
    has_next = (row < grid_rows - 1, col < grid_cols - 1)
    nexts = ((row + 1, col), (row, col + 1))
    prevs = ((row - 1, col), (row, col - 1))
    turn = row % 2
    near = pair % 2
    line_prev = (row - group, col), (row + 1 - 2 * turn, col - (1 - turn) * (3 - 2 * near))
    line_next = (row + group, col), (row + 1 - 2 * turn, col + turn * (1 + 2 * near))
    line_has_prev = (first_row > 0, own_col > 0)
    line_has_next = (first_row + group < grid_rows, own_col < grid_cols - 1)

    barrier = pltpu.get_barrier_semaphore()

    def greet(flag, target):
        @pl.when(flag)
        def _():
            pl.semaphore_signal(
                barrier, inc=1, device_id=device(*target), device_id_type=MESH
            )

    def number(flag):
        return flag.astype(jnp.int32)

    before = jnp.maximum(col - 1, 0)
    for s in range(count):
        greet(other(*solver(s)), solver(s))
        greet(jnp.logical_and(col > 0, other(*solver(s, before))), solver(s, before))
    for axis in range(2):
        greet(has_next[axis], nexts[axis])

    @pl.when(solves)
    def _():
        for k in range(group):
            greet(other(*home(k)), home(k))
        for axis in range(2):
            greet(line_has_prev[axis], line_prev[axis])

    load_inputs()

    def copy(source, target, sent, received, peer):
        return pltpu.make_async_remote_copy(
            src_ref=source,
            dst_ref=target,
            send_sem=sent,
            recv_sem=received,
            device_id=device(*peer),
            device_id_type=MESH,
        )

    def give_medium(s):
        return copy(
            contrast, medium_in.at[place], medium_send.at[s], medium_recv.at[place], solver(s)
        )

    def give_free(s):
        return copy(
            free_out.at[s], free_in.at[place], free_send.at[s], free_recv.at[place], solver(s)
        )

    def take_medium(k):
        return copy(
            contrast, medium_in.at[k], medium_send.at[0], medium_recv.at[k], home(k)
        )

    def take_free(k):
        return copy(free_out.at[0], free_in.at[k], free_send.at[0], free_recv.at[k], home(k))

    def give_home(k):
        return copy(
            x_line.at[k],
            inbound.at[own_rhs, 0],
            home_send.at[k, 0],
            home_recv.at[own_rhs, 0],
            home(k),
        )

    def pass_side(k):
        return copy(
            y_out.at[k],
            inbound.at[own_rhs, 1],
            home_send.at[k, 1],
            home_recv.at[own_rhs, 1],
            side(k),
        )

    def take_home(s, axis):
        line = (x_line, y_out)[axis]
        return copy(
            line.at[0], inbound.at[s, axis], home_send.at[0, axis], home_recv.at[s, axis],
            solver(s),
        )

    pass_x = copy(x_line.at[group], x_line.at[0], x_send, x_recv, line_next[0])

    def pass_y(k):
        return copy(y_out.at[k], y_line.at[k], y_send.at[k], y_recv.at[k], line_next[1])

    def backward(s, axis):
        source, target = ((back_x, after_x), (back_y, after_y))[axis]
        return copy(
            source.at[s], target.at[s], back_send.at[s, axis], back_recv.at[s, axis], prevs[axis]
        )

    vertical = (ver_ref, ver2_ref)

    def physical_of(values):
        return to_physical(along_z(values, vertical), outw_ref, size_x)

    def modes_of(values):
        return to_modes(along_z(values, vertical), inv_ref, size_x)

    def modes(values):
        return times(lam_r[...], lam_i[...], values)

    def load(ref):
        return jnp.concatenate([ref[0], ref[1]], axis=1)

    def save(ref, values):
        ref[0] = values[:, :size_z]
        ref[1] = values[:, size_z:]

    def through(factor, values):
        return times(factor[0], factor[1], values)

    def factors(target, scaled):
        target[0] = scaled - edge_ref[...]
        target[1] = DAMPING * scaled

    def sweeps(hat, work, factor, keep=None):
        save(work, modes(load(hat)))
        for sweep in range(2):
            physical = through(factor, physical_of(load(work)))
            if keep is not None:
                save(keep, physical)
            save(work, modes(load(hat) + modes_of(physical)))

    def traces_of(work):
        return by_part(gather_ref[...], load(work))

    def spread_of(first, second):
        return by_part(spread_ref[...], jnp.concatenate([first, second], axis=0))

    half = 2 * size_y
    upper = size_y // 2
    for t in range(upper):
        contrast[pl.ds(t, size_x, stride=size_y), :] = KAPPA * (
            slow_ref[pl.ds(t, size_x, stride=size_y), :] - 1.0
        )
        contrast[pl.ds(upper + t, size_x, stride=size_y), :] = KAPPA * (
            slow_ref[pl.ds(size_y - 1 - t, size_x, stride=size_y), :] - 1.0
        )
    factors(medium, contrast[...])

    points = cells_ref.shape[1]
    row_ids = lax.broadcasted_iota(jnp.int32, (rows, points), 0)
    in_row = row_ids % size_y
    in_row = jnp.where(in_row < upper, in_row, size_y + upper - 1 - in_row)
    row_ids = row_ids - row_ids % size_y + in_row
    lane_ids = lax.broadcasted_iota(jnp.int32, (size_z, points), 0)

    def fold(s):
        for c in range(2):
            for t in range(upper):
                low = pl.ds(t, size_x, stride=size_y)
                inner[s, c, low, :] = rs_ref[s, c, low, :]
                high = pl.ds(size_y - 1 - t, size_x, stride=size_y)
                inner[s, c, pl.ds(upper + t, size_x, stride=size_y), :] = rs_ref[s, c, high, :]

    def forcing(s):
        fold(s)
        flat = cells_ref[pl.ds(s, 1), :]
        at_x = flat // (size_y * grid_cols * size_z) - row * size_x
        at_y = flat // size_z % (size_y * grid_cols) - col * size_y
        inside = jnp.logical_and(
            jnp.logical_and(at_x >= 0, at_x < size_x), jnp.logical_and(at_y >= 0, at_y < size_y)
        )
        at_row = jnp.where(inside, at_x * size_y + at_y, -1)
        where_row = jnp.where(row_ids == at_row, 1.0, 0.0).astype(BF16)
        hit_z = lane_ids == flat % size_z
        outs = []
        for c in range(2):
            rest = jnp.where(hit_z, amp_ref[s, c : c + 1, :], 0.0)
            total = inner[s, c]
            for term in range(3):
                part = rest.astype(BF16)
                rest = rest - part.astype(F32)
                total = total + lax.dot_general(
                    where_row, part, (((1,), (1,)), ((), ())), preferred_element_type=F32
                )
            outs.append(total)
        return jnp.concatenate(outs, axis=1)

    peers = sum(number(other(*solver(s))) for s in range(count))
    peers = peers + sum(number(flag) for flag in has_prev)
    line_peers = sum(number(other(*home(k))) for k in range(group))
    line_peers = line_peers + sum(number(flag) for flag in line_has_next)
    line_peers = line_peers + sum(
        number(jnp.logical_and(line_has_next[1], other(*side(k)))) for k in range(group)
    )

    def if_other(flag_target, action):
        @pl.when(other(*flag_target))
        def _():
            action()

    early = jnp.logical_and(col < grid_cols // 2, jnp.logical_or(place < 2, col == 0))
    corner = jnp.logical_and(row == 0, col == 0)

    @pl.when(col == 0)
    def _():
        inbound[:, 1] = jnp.zeros_like(inbound[:, 1])

    @pl.when(solves)
    def _():
        @pl.when(first_row == 0)
        def _():
            x_line[0] = jnp.zeros_like(x_line[0])

        @pl.when(own_col == 0)
        def _():
            y_line[...] = jnp.zeros_like(y_line)

    def rank(step):
        return jnp.where(place < 2, count - 1 - step, step)

    def open_sends():
        pl.semaphore_wait(barrier, peers + jnp.where(solves, line_peers, 0))
        for s in range(count):
            @pl.when(jnp.logical_and(early, jnp.logical_and(other(*solver(s)), ~corner)))
            def _():
                give_medium(s).start()

        if_other(solver(rank(0)), give_free(rank(0)).start)

    def prepare(step, _):
        s = rank(step)

        @pl.when(step == 1)
        def _():
            open_sends()

        save(fhat.at[s], modes_of(forcing(s)))
        sweeps(fhat.at[s], spec.at[s], medium)
        out = traces_of(spec.at[s])
        free_out[s, 0] = out[:half]
        free_out[s, 1] = out[half:]

        @pl.when(jnp.logical_and(step == 1, other(*solver(s))))
        def _():
            give_free(s).start()
        return 0

    lax.fori_loop(0, count, prepare, 0)
    for s in range(count):
        @pl.when(jnp.logical_and(~early, other(*solver(s))))
        def _():
            give_medium(s).start()

    def advance(k, _):
        tile_row, tile_col = home(k)
        mine = same(tile_row, tile_col)

        start = jnp.logical_and(tile_row == 0, tile_col == 0)
        end = jnp.logical_and(tile_row == grid_rows - 1, tile_col == grid_cols - 1)

        @pl.when(mine)
        def _():
            free_in[k] = free_out[own_rhs]
            line_medium[...] = medium[...]

        @pl.when(jnp.logical_not(jnp.logical_or(mine, start)))
        def _():
            take_medium(k).wait_recv()
            factors(line_medium, medium_in[k])

        @pl.when(jnp.logical_and(k == 0, first_row > 0))
        def _():
            pass_x.wait_recv()

        @pl.when(mine)
        def _():
            inbound[own_rhs, 0] = x_line[k]

        @pl.when(jnp.logical_not(mine))
        def _():
            give_home(k).start()

        @pl.when(own_col > 0)
        def _():
            pass_y(k).wait_recv()

        @pl.when(jnp.logical_not(jnp.logical_or(start, end)))
        def _():
            save(bound_hat, spread_of(x_line[k], y_line[k]))
            sweeps(bound_hat, bound_spec, line_medium)
            out = traces_of(bound_spec)
            x_line[k + 1] = out[:half]
            y_out[k] = out[half:]

        @pl.when(start)
        def _():
            x_line[k + 1] = jnp.zeros_like(x_line[k])
            y_out[k] = jnp.zeros_like(y_out[k])

        @pl.when(jnp.logical_not(mine))
        def _():
            take_free(k).wait_recv()

        @pl.when(jnp.logical_not(end))
        def _():
            x_line[k + 1] += free_in[k, 0]
            y_out[k] += free_in[k, 1]

        @pl.when(jnp.logical_and(k == group - 1, line_has_next[0]))
        def _():
            pass_x.start()

        @pl.when(line_has_next[1])
        def _():
            pass_y(k).start()

            @pl.when(other(*side(k)))
            def _():
                pass_side(k).start()

            @pl.when(same(*side(k)))
            def _():
                inbound[own_rhs, 1] = y_out[k]
        return 0

    @pl.when(solves)
    def _():
        lax.fori_loop(0, group, advance, 0)

    def unfold(target, source, s, c):
        for t in range(upper):
            low = pl.ds(t, size_x, stride=size_y)
            target[s, c, low, :] = source[s, c, low, :]
            high = pl.ds(size_y - 1 - t, size_x, stride=size_y)
            target[s, c, high, :] = source[s, c, pl.ds(upper + t, size_x, stride=size_y), :]

    def finish(step, _):
        s = count - 1 - step

        @pl.when(other(*solver(s)))
        def _():
            take_home(s, 0).wait_recv()

        @pl.when(jnp.logical_and(col > 0, other(*solver(s, before))))
        def _():
            take_home(s, 1).wait_recv()

        save(fhat.at[s], load(fhat.at[s]) + spread_of(inbound[s, 0], inbound[s, 1]))
        sweeps(fhat.at[s], spec.at[s], medium, inner.at[s])
        wave = physical_of(load(spec.at[s]))
        save(inner.at[s], through(medium, wave) - load(inner.at[s]))
        save(spec.at[s], wave)
        for c in range(2):
            lanes = slice(c * size_z, (c + 1) * size_z)
            unfold(wave_ref, spec, s, c)
            back_x[s, :, lanes] = wave_ref[s, c, :half]
            for l in range(2):
                back_y[s, l, :, lanes] = wave_ref[s, c, pl.ds(l, size_x, stride=size_y), :]
        for axis in range(2):
            @pl.when(has_prev[axis])
            def _():
                backward(s, axis).start()
        return 0

    lax.fori_loop(0, count, finish, 0)

    def close(step, _):
        s = count - 1 - step
        for c in range(2):
            unfold(resid_ref, inner, s, c)

        @pl.when(has_next[0])
        def _():
            backward(s, 0).wait_recv()
            near = after_x[s, :size_y]
            far = after_x[s, size_y:]
            for c in range(2):
                lanes = slice(c * size_z, (c + 1) * size_z)
                resid_ref[s, c, rows - 2 * size_y : rows - size_y] -= near[:, lanes] / 12.0
                resid_ref[s, c, rows - size_y :] += (16.0 * near - far)[:, lanes] / 12.0

        @pl.when(has_next[1])
        def _():
            backward(s, 1).wait_recv()
            near = after_y[s, 0]
            far = after_y[s, 1]
            for c in range(2):
                lanes = slice(c * size_z, (c + 1) * size_z)
                below = pl.ds(size_y - 2, size_x, stride=size_y)
                last = pl.ds(size_y - 1, size_x, stride=size_y)
                resid_ref[s, c, below, :] = resid_ref[s, c, below, :] - near[:, lanes] / 12.0
                resid_ref[s, c, last, :] = (
                    resid_ref[s, c, last, :] + (16.0 * near - far)[:, lanes] / 12.0
                )

        @pl.when(other(*solver(s)))
        def _():
            give_free(s).wait_send()

        @pl.when(jnp.logical_and(other(*solver(s)), ~corner))
        def _():
            give_medium(s).wait_send()

        for axis in range(2):
            @pl.when(has_prev[axis])
            def _():
                backward(s, axis).wait_send()
        return 0

    lax.fori_loop(0, count, close, 0)


    @pl.when(solves)
    def _():
        @pl.when(line_has_next[0])
        def _():
            pass_x.wait_send()

        def settle(k, _):
            @pl.when(other(*home(k)))
            def _():
                give_home(k).wait_send()

            @pl.when(line_has_next[1])
            def _():
                pass_y(k).wait_send()

                @pl.when(other(*side(k)))
                def _():
                    pass_side(k).wait_send()
            return 0

        lax.fori_loop(0, group, settle, 0)


def staged(sizes, inputs, *refs):
    sources, refs = refs[:inputs], refs[inputs:]
    wave, resid, refs = refs[0], refs[1], refs[2:]
    targets, refs = refs[:inputs], refs[inputs:]
    in_sem, refs = refs[0], refs[1:]

    def load_inputs():
        copies = [
            pltpu.make_async_copy(source, target, in_sem.at[i])
            for i, (source, target) in enumerate(zip(sources, targets))
        ]
        for copy in copies:
            copy.start()
        for copy in copies:
            copy.wait()

    kernel(load_inputs, *sizes, *targets, wave, resid, *refs)


def solution(mesh):
    grid_rows, grid_cols = mesh.shape["gx"], mesh.shape["gy"]
    group = 8

    def body(right_side, slowness, source_cells, source_amplitudes):
        count, parts, size_x, size_y, size_z = right_side.shape
        rows = size_x * size_y
        wide = 2 * size_z
        tables = build_tables(size_x, size_y, size_z)
        dma = pltpu.SemaphoreType.DMA

        def field(*lead):
            return pltpu.VMEM((*lead, 2, rows, size_z), F32)

        def traces(*lead):
            return pltpu.VMEM((*lead, 2 * size_y, wide), F32)

        whole = pl.BlockSpec(memory_space=pl.ANY)
        block = jax.ShapeDtypeStruct((count, parts, rows, size_z), F32)
        operands = (
            right_side.reshape(count, parts, rows, size_z),
            slowness.reshape(rows, size_z),
            source_cells,
            source_amplitudes.transpose(0, 2, 1),
            *[jnp.asarray(t) for t in tables],
        )
        sizes = (grid_rows, grid_cols, (size_x, size_y, size_z), group)
        wave, resid = pl.pallas_call(
            functools.partial(staged, sizes, len(operands)),
            out_shape=(pltpu.VMEM(block.shape, F32), pltpu.VMEM(block.shape, F32)),
            in_specs=[whole] * len(operands),
            out_specs=(pl.BlockSpec(memory_space=pltpu.VMEM),) * 2,
            scratch_shapes=[pltpu.VMEM(o.shape, o.dtype) for o in operands]
            + [dma((len(operands),))]
            + [
                field(count),
                field(count),
                field(count),
                pltpu.VMEM((rows, size_z), F32),
                field(),
                traces(count, 2),
                traces(count, 2),
                traces(count),
                pltpu.VMEM((count, 2, size_x, wide), F32),
                traces(count),
                pltpu.VMEM((count, 2, size_x, wide), F32),
                pltpu.VMEM((group, rows, size_z), F32),
                traces(group, 2),
                traces(group + 1),
                traces(group),
                traces(group),
                field(),
                field(),
                field(),
                dma((count,)),
                dma((group,)),
                dma((count,)),
                dma((group,)),
                dma((group, 2)),
                dma((count, 2)),
                dma,
                dma,
                dma((group,)),
                dma((group,)),
                dma((count, 2)),
                dma((count, 2)),
            ],
            compiler_params=pltpu.CompilerParams(collective_id=0, has_side_effects=True),
        )(*operands)
        shape = (count, parts, size_x, size_y, size_z)
        return (wave.reshape(shape), resid.reshape(shape))

    return jax.shard_map(
        body,
        mesh=mesh,
        in_specs=(P(None, None, "gx", "gy", None), P("gx", "gy", None), P(), P()),
        out_specs=(P(None, None, "gx", "gy", None), P(None, None, "gx", "gy", None)),
        check_vma=False,
    )
```

```python
import functools

import jax
import jax.numpy as jnp
import numpy as np
from jax import lax
from jax.experimental import pallas as pl
from jax.experimental.pallas import tpu as pltpu
from jax.sharding import PartitionSpec as P

KAPPA = 0.12
DAMPING = 0.3
MESH = pl.DeviceIdType.MESH
F32 = jnp.float32
BF16 = jnp.bfloat16


def split_table(table):
    high = np.asarray(table, np.float32).astype(BF16)
    low = (np.asarray(table, np.float64) - high.astype(np.float64)).astype(np.float32).astype(BF16)
    return high, low


def stacked(table):
    high, low = split_table(table)
    return np.concatenate([high, low, high], axis=1)


def sine_basis(length):
    positions = np.arange(1, length + 1, dtype=np.float64)
    angles = positions * (np.pi / (length + 1))
    return np.sqrt(2.0 / (length + 1)) * np.sin(angles[:, None] * positions[None, :]), angles


def build_tables(size_x, size_y, cells_z):
    sine_x, angle_x = sine_basis(size_x)
    sine_y, angle_y = sine_basis(size_y)
    sine_z, angle_z = sine_basis(cells_z)
    symbol_x = 2.5 - 8.0 / 3.0 * np.cos(angle_x) + np.cos(2.0 * angle_x) / 6.0
    symbol_y = 2.5 - 8.0 / 3.0 * np.cos(angle_y) + np.cos(2.0 * angle_y) / 6.0
    symbol_z = 2.0 - 2.0 * np.cos(angle_z)
    real_part = symbol_x[:, None, None] + symbol_y[None, :, None] + symbol_z - KAPPA
    denominator = real_part * real_part + (KAPPA * DAMPING) ** 2
    inverse_real = (real_part / denominator).reshape(size_x * size_y, cells_z).astype(np.float32)
    inverse_imag = (KAPPA * DAMPING / denominator).reshape(size_x * size_y, cells_z)
    inverse_imag = inverse_imag.astype(np.float32)
    half_x, half_y = size_x // 2, size_y // 2
    order = np.arange(size_x * size_y).reshape(half_x, 2, half_y, 2)
    order = order.transpose(1, 3, 0, 2).reshape(-1)
    folded = np.arange(size_x * size_y).reshape(size_x, 2, half_y)
    folded[:, 1] = folded[:, 1, ::-1]
    folded = folded.reshape(-1)
    blocks = [
        np.kron(sine_x[:half_x, a::2], sine_y[:half_y, b::2]) for a in range(2) for b in range(2)
    ]
    outward = np.stack([stacked(block) for block in blocks])
    inverse = np.stack([stacked(block.T) for block in blocks])
    high, low = split_table(sine_z)
    vertical = np.concatenate([np.concatenate([high, low], axis=1)] * 2, axis=0)
    eye_x = np.eye(size_x)
    eye_y = np.eye(size_y)

    def inward(sine):
        return (-sine[:, 0] / 12.0, (16.0 * sine[:, 0] - sine[:, 1]) / 12.0)

    spread = [np.kron(v[:, None], eye_y) for v in inward(sine_x)]
    spread += [np.kron(eye_x, v[:, None]) for v in inward(sine_y)]
    gather = [np.kron(sine_x[size_x - 2 + l][None, :], eye_y) for l in range(2)]
    gather += [np.kron(eye_x, sine_y[size_y - 2 + l][None, :]) for l in range(2)]
    edge_x = np.zeros(size_x)
    edge_x[[0, -1]] = 1.0 / 12.0
    edge_y = np.zeros(size_y)
    edge_y[[0, -1]] = 1.0 / 12.0
    edges = np.repeat((edge_x[:, None] + edge_y[None, :]).reshape(-1, 1), cells_z, axis=1)
    return (
        outward,
        inverse,
        vertical,
        vertical,
        stacked(np.concatenate(spread, axis=1)[order]),
        stacked(np.concatenate(gather, axis=0)[:, order]),
        inverse_real[order],
        inverse_imag[order],
        edges[folded].astype(np.float32),
    )


def split(values):
    high = values.astype(BF16)
    return high, (values - high.astype(F32)).astype(BF16)


def product(table, values):
    high, low = split(values)
    return jnp.dot(
        table, jnp.concatenate([high, high, low], axis=0), preferred_element_type=F32
    )


def by_part(table, values):
    half = values.shape[1] // 2
    return jnp.concatenate(
        [product(table, values[:, p * half : (p + 1) * half]) for p in range(2)], axis=1
    )


def along_z(values, vertical):
    half = values.shape[1] // 2
    outs = []
    for part in range(2):
        high, low = split(values[:, part * half : (part + 1) * half])
        both = jnp.concatenate([high, low], axis=1)
        mixed = jnp.dot(both, vertical[part][...], preferred_element_type=F32)
        outs.append(mixed[:, :half] + mixed[:, half:])
    return jnp.concatenate(outs, axis=1)


def to_physical(values, tables, size_x):
    rows = values.shape[0] // 4
    step = rows * 2 // size_x
    even, odd, even_odd, odd_odd = [
        product(tables[p], values[p * rows : (p + 1) * rows]) for p in range(4)
    ]
    near, far = even + odd, even - odd
    near_odd, far_odd = even_odd + odd_odd, even_odd - odd_odd
    first = (near + near_odd, far + far_odd)
    last = (near - near_odd, far - far_odd)
    slices = [slice(i * step, (i + 1) * step) for i in range(size_x // 2)]
    pieces = [part[at] for at in slices for part in first]
    pieces += [part[at] for at in slices[::-1] for part in last]
    return jnp.concatenate(pieces, axis=0)


def to_modes(values, tables, size_x):
    step = values.shape[0] // (2 * size_x)

    def quadrant(first, half):
        ids = range(size_x // 2) if first else range(size_x - 1, size_x // 2 - 1, -1)
        starts = [(2 * i + half) * step for i in ids]
        return jnp.concatenate([values[at : at + step] for at in starts], axis=0)

    top = (quadrant(True, 0), quadrant(True, 1))
    bottom = (quadrant(False, 0), quadrant(False, 1))
    even = [t + b for t, b in zip(top, bottom)]
    odd = [t - b for t, b in zip(top, bottom)]
    folded = [even[0] + even[1], even[0] - even[1], odd[0] + odd[1], odd[0] - odd[1]]
    return jnp.concatenate([product(tables[p], folded[p]) for p in range(4)], axis=0)


def times(real, imag, values):
    half = values.shape[1] // 2
    first, second = values[:, :half], values[:, half:]
    return jnp.concatenate(
        [real * first - imag * second, real * second + imag * first], axis=1
    )


def kernel(
    load_inputs, grid_rows, grid_cols, cells, group,
    rs_ref, slow_ref, cells_ref, amp_ref,
    outw_ref, inv_ref, ver_ref, ver2_ref, spread_ref, gather_ref, lam_r, lam_i, edge_ref,
    wave_ref, resid_ref,
    fhat, spec, inner, contrast, medium, free_out, inbound, back_x, back_y, after_x, after_y,
    medium_in, free_in, x_line, y_line, y_out, bound_hat, bound_spec, line_medium,
    medium_send, medium_recv, free_send, free_recv, home_send, home_recv,
    x_send, x_recv, y_send, y_recv, back_send, back_recv,
):
    size_x, size_y, size_z = cells
    rows = size_x * size_y
    count = rs_ref.shape[0]
    row = lax.axis_index("gx")
    col = lax.axis_index("gy")
    place = row % group
    first_row = row - place
    odd = col % 2
    pair = col // 2
    last = first_row + group >= grid_rows
    shift = jnp.where(last, group - 4, 0)
    seat = place - shift
    solves = jnp.logical_and(odd != pair % 2, jnp.logical_and(seat >= 0, seat < 4))
    own_rhs = jnp.clip(seat, 0, 3) // 2
    own_col = 2 * pair + row % 2

    def device(gx, gy):
        return {"gx": gx, "gy": gy}

    def same(gx, gy):
        return jnp.logical_and(gx == row, gy == col)

    def other(gx, gy):
        return jnp.logical_not(same(gx, gy))

    def solver(s, tile_col=col):
        group_col = tile_col - tile_col % 2
        return first_row + shift + 2 * s + tile_col % 2, group_col + 1 - group_col // 2 % 2

    def home(k):
        return first_row + k, own_col

    def side(k):
        return first_row + k, own_col + 1

    has_prev = (row > 0, col > 0)
    has_next = (row < grid_rows - 1, col < grid_cols - 1)
    nexts = ((row + 1, col), (row, col + 1))
    prevs = ((row - 1, col), (row, col - 1))
    turn = row % 2
    near = pair % 2
    next_shift = jnp.where(first_row + 2 * group >= grid_rows, group - 4, 0)
    line_prev = (row - group - shift, col), (row + 1 - 2 * turn, col - (1 - turn) * (3 - 2 * near))
    line_next = (row + group + next_shift - shift, col), (row + 1 - 2 * turn, col + turn * (1 + 2 * near))
    line_has_prev = (first_row > 0, own_col > 0)
    line_has_next = (first_row + group < grid_rows, own_col < grid_cols - 1)

    barrier = pltpu.get_barrier_semaphore()

    def greet(flag, target):
        @pl.when(flag)
        def _():
            pl.semaphore_signal(
                barrier, inc=1, device_id=device(*target), device_id_type=MESH
            )

    def number(flag):
        return flag.astype(jnp.int32)

    before = jnp.maximum(col - 1, 0)
    for s in range(count):
        greet(other(*solver(s)), solver(s))
        greet(jnp.logical_and(col > 0, other(*solver(s, before))), solver(s, before))
    for axis in range(2):
        greet(has_next[axis], nexts[axis])

    @pl.when(solves)
    def _():
        for k in range(group):
            greet(other(*home(k)), home(k))
        for axis in range(2):
            greet(line_has_prev[axis], line_prev[axis])

    load_inputs()

    def copy(source, target, sent, received, peer):
        return pltpu.make_async_remote_copy(
            src_ref=source,
            dst_ref=target,
            send_sem=sent,
            recv_sem=received,
            device_id=device(*peer),
            device_id_type=MESH,
        )

    def give_medium(s):
        return copy(
            contrast, medium_in.at[place], medium_send.at[s], medium_recv.at[place], solver(s)
        )

    def give_free(s):
        return copy(
            free_out.at[s], free_in.at[place], free_send.at[s], free_recv.at[place], solver(s)
        )

    def take_medium(k):
        return copy(
            contrast, medium_in.at[k], medium_send.at[0], medium_recv.at[k], home(k)
        )

    def take_free(k):
        return copy(free_out.at[0], free_in.at[k], free_send.at[0], free_recv.at[k], home(k))

    def give_home(k):
        return copy(
            x_line.at[k],
            inbound.at[own_rhs, 0],
            home_send.at[k, 0],
            home_recv.at[own_rhs, 0],
            home(k),
        )

    def pass_side(k):
        return copy(
            y_out.at[k],
            inbound.at[own_rhs, 1],
            home_send.at[k, 1],
            home_recv.at[own_rhs, 1],
            side(k),
        )

    def take_home(s, axis):
        line = (x_line, y_out)[axis]
        return copy(
            line.at[0], inbound.at[s, axis], home_send.at[0, axis], home_recv.at[s, axis],
            solver(s),
        )

    pass_x = copy(x_line.at[group], x_line.at[0], x_send, x_recv, line_next[0])

    def pass_y(k):
        return copy(y_out.at[k], y_line.at[k], y_send.at[k], y_recv.at[k], line_next[1])

    def backward(s, axis):
        source, target = ((back_x, after_x), (back_y, after_y))[axis]
        return copy(
            source.at[s], target.at[s], back_send.at[s, axis], back_recv.at[s, axis], prevs[axis]
        )

    vertical = (ver_ref, ver2_ref)

    def physical_of(values):
        return to_physical(along_z(values, vertical), outw_ref, size_x)

    def modes_of(values):
        return to_modes(along_z(values, vertical), inv_ref, size_x)

    def modes(values):
        return times(lam_r[...], lam_i[...], values)

    def load(ref):
        return jnp.concatenate([ref[0], ref[1]], axis=1)

    def save(ref, values):
        ref[0] = values[:, :size_z]
        ref[1] = values[:, size_z:]

    def through(factor, values):
        return times(factor[0], factor[1], values)

    def factors(target, scaled):
        target[0] = scaled - edge_ref[...]
        target[1] = DAMPING * scaled

    def sweeps(hat, work, factor, keep=None):
        save(work, modes(load(hat)))
        for sweep in range(2):
            physical = through(factor, physical_of(load(work)))
            if keep is not None:
                save(keep, physical)
            save(work, modes(load(hat) + modes_of(physical)))

    def traces_of(work):
        return by_part(gather_ref[...], load(work))

    def spread_of(first, second):
        return by_part(spread_ref[...], jnp.concatenate([first, second], axis=0))

    half = 2 * size_y
    upper = size_y // 2
    for t in range(upper):
        contrast[pl.ds(t, size_x, stride=size_y), :] = KAPPA * (
            slow_ref[pl.ds(t, size_x, stride=size_y), :] - 1.0
        )
        contrast[pl.ds(upper + t, size_x, stride=size_y), :] = KAPPA * (
            slow_ref[pl.ds(size_y - 1 - t, size_x, stride=size_y), :] - 1.0
        )
    factors(medium, contrast[...])

    points = cells_ref.shape[1]
    row_ids = lax.broadcasted_iota(jnp.int32, (rows, points), 0)
    in_row = row_ids % size_y
    in_row = jnp.where(in_row < upper, in_row, size_y + upper - 1 - in_row)
    row_ids = row_ids - row_ids % size_y + in_row
    lane_ids = lax.broadcasted_iota(jnp.int32, (size_z, points), 0)

    def fold(s):
        for c in range(2):
            for t in range(upper):
                low = pl.ds(t, size_x, stride=size_y)
                inner[s, c, low, :] = rs_ref[s, c, low, :]
                high = pl.ds(size_y - 1 - t, size_x, stride=size_y)
                inner[s, c, pl.ds(upper + t, size_x, stride=size_y), :] = rs_ref[s, c, high, :]

    def forcing(s):
        fold(s)
        flat = cells_ref[pl.ds(s, 1), :]
        at_x = flat // (size_y * grid_cols * size_z) - row * size_x
        at_y = flat // size_z % (size_y * grid_cols) - col * size_y
        inside = jnp.logical_and(
            jnp.logical_and(at_x >= 0, at_x < size_x), jnp.logical_and(at_y >= 0, at_y < size_y)
        )
        at_row = jnp.where(inside, at_x * size_y + at_y, -1)
        where_row = jnp.where(row_ids == at_row, 1.0, 0.0).astype(BF16)
        hit_z = lane_ids == flat % size_z
        outs = []
        for c in range(2):
            rest = jnp.where(hit_z, amp_ref[s, c : c + 1, :], 0.0)
            total = inner[s, c]
            for term in range(3):
                part = rest.astype(BF16)
                rest = rest - part.astype(F32)
                total = total + lax.dot_general(
                    where_row, part, (((1,), (1,)), ((), ())), preferred_element_type=F32
                )
            outs.append(total)
        return jnp.concatenate(outs, axis=1)

    peers = sum(number(other(*solver(s))) for s in range(count))
    peers = peers + sum(number(flag) for flag in has_prev)
    line_peers = sum(number(other(*home(k))) for k in range(group))
    line_peers = line_peers + sum(number(flag) for flag in line_has_next)
    line_peers = line_peers + sum(
        number(jnp.logical_and(line_has_next[1], other(*side(k)))) for k in range(group)
    )

    def if_other(flag_target, action):
        @pl.when(other(*flag_target))
        def _():
            action()

    early = jnp.logical_and(col < grid_cols // 2, jnp.logical_or(place < 2, jnp.logical_and(col == 0, place < 4)))
    corner = jnp.logical_and(row == 0, col == 0)

    @pl.when(col == 0)
    def _():
        inbound[:, 1] = jnp.zeros_like(inbound[:, 1])

    @pl.when(solves)
    def _():
        @pl.when(first_row == 0)
        def _():
            x_line[0] = jnp.zeros_like(x_line[0])

        @pl.when(own_col == 0)
        def _():
            y_line[...] = jnp.zeros_like(y_line)

    def rank(step):
        return jnp.where(place < 2, count - 1 - step, step)

    def open_sends():
        pl.semaphore_wait(barrier, peers + jnp.where(solves, line_peers, 0))
        for s in range(count):
            @pl.when(jnp.logical_and(early, jnp.logical_and(other(*solver(s)), ~corner)))
            def _():
                give_medium(s).start()

        if_other(solver(rank(0)), give_free(rank(0)).start)

    def prepare(step, _):
        s = rank(step)

        @pl.when(step == 1)
        def _():
            open_sends()

        save(fhat.at[s], modes_of(forcing(s)))
        sweeps(fhat.at[s], spec.at[s], medium)
        out = traces_of(spec.at[s])
        free_out[s, 0] = out[:half]
        free_out[s, 1] = out[half:]

        @pl.when(jnp.logical_and(step == 1, other(*solver(s))))
        def _():
            give_free(s).start()
        return 0

    lax.fori_loop(0, count, prepare, 0)
    for s in range(count):
        @pl.when(jnp.logical_and(~early, other(*solver(s))))
        def _():
            give_medium(s).start()

    def advance(k, _):
        tile_row, tile_col = home(k)
        mine = same(tile_row, tile_col)

        start = jnp.logical_and(tile_row == 0, tile_col == 0)
        end = jnp.logical_and(tile_row == grid_rows - 1, tile_col == grid_cols - 1)

        @pl.when(mine)
        def _():
            free_in[k] = free_out[own_rhs]
            line_medium[...] = medium[...]

        @pl.when(jnp.logical_not(jnp.logical_or(mine, start)))
        def _():
            take_medium(k).wait_recv()
            factors(line_medium, medium_in[k])

        @pl.when(jnp.logical_and(k == 0, first_row > 0))
        def _():
            pass_x.wait_recv()

        @pl.when(mine)
        def _():
            inbound[own_rhs, 0] = x_line[k]

        @pl.when(jnp.logical_not(mine))
        def _():
            give_home(k).start()

        @pl.when(own_col > 0)
        def _():
            pass_y(k).wait_recv()

        @pl.when(jnp.logical_not(jnp.logical_or(start, end)))
        def _():
            save(bound_hat, spread_of(x_line[k], y_line[k]))
            sweeps(bound_hat, bound_spec, line_medium)
            out = traces_of(bound_spec)
            x_line[k + 1] = out[:half]
            y_out[k] = out[half:]

        @pl.when(start)
        def _():
            x_line[k + 1] = jnp.zeros_like(x_line[k])
            y_out[k] = jnp.zeros_like(y_out[k])

        @pl.when(jnp.logical_not(mine))
        def _():
            take_free(k).wait_recv()

        @pl.when(jnp.logical_not(end))
        def _():
            x_line[k + 1] += free_in[k, 0]
            y_out[k] += free_in[k, 1]

        @pl.when(jnp.logical_and(k == group - 1, line_has_next[0]))
        def _():
            pass_x.start()

        @pl.when(line_has_next[1])
        def _():
            pass_y(k).start()

            @pl.when(other(*side(k)))
            def _():
                pass_side(k).start()

            @pl.when(same(*side(k)))
            def _():
                inbound[own_rhs, 1] = y_out[k]
        return 0

    @pl.when(solves)
    def _():
        lax.fori_loop(0, group, advance, 0)

    def unfold(target, source, s, c):
        for t in range(upper):
            low = pl.ds(t, size_x, stride=size_y)
            target[s, c, low, :] = source[s, c, low, :]
            high = pl.ds(size_y - 1 - t, size_x, stride=size_y)
            target[s, c, high, :] = source[s, c, pl.ds(upper + t, size_x, stride=size_y), :]

    def finish(step, _):
        s = count - 1 - step

        @pl.when(other(*solver(s)))
        def _():
            take_home(s, 0).wait_recv()

        @pl.when(jnp.logical_and(col > 0, other(*solver(s, before))))
        def _():
            take_home(s, 1).wait_recv()

        save(fhat.at[s], load(fhat.at[s]) + spread_of(inbound[s, 0], inbound[s, 1]))
        sweeps(fhat.at[s], spec.at[s], medium, inner.at[s])
        wave = physical_of(load(spec.at[s]))
        save(inner.at[s], through(medium, wave) - load(inner.at[s]))
        save(spec.at[s], wave)
        for c in range(2):
            lanes = slice(c * size_z, (c + 1) * size_z)
            unfold(wave_ref, spec, s, c)
            back_x[s, :, lanes] = wave_ref[s, c, :half]
            for l in range(2):
                back_y[s, l, :, lanes] = wave_ref[s, c, pl.ds(l, size_x, stride=size_y), :]
        for axis in range(2):
            @pl.when(has_prev[axis])
            def _():
                backward(s, axis).start()
        return 0

    lax.fori_loop(0, count, finish, 0)

    def close(step, _):
        s = count - 1 - step
        for c in range(2):
            unfold(resid_ref, inner, s, c)

        @pl.when(has_next[0])
        def _():
            backward(s, 0).wait_recv()
            near = after_x[s, :size_y]
            far = after_x[s, size_y:]
            for c in range(2):
                lanes = slice(c * size_z, (c + 1) * size_z)
                resid_ref[s, c, rows - 2 * size_y : rows - size_y] -= near[:, lanes] / 12.0
                resid_ref[s, c, rows - size_y :] += (16.0 * near - far)[:, lanes] / 12.0

        @pl.when(has_next[1])
        def _():
            backward(s, 1).wait_recv()
            near = after_y[s, 0]
            far = after_y[s, 1]
            for c in range(2):
                lanes = slice(c * size_z, (c + 1) * size_z)
                below = pl.ds(size_y - 2, size_x, stride=size_y)
                last = pl.ds(size_y - 1, size_x, stride=size_y)
                resid_ref[s, c, below, :] = resid_ref[s, c, below, :] - near[:, lanes] / 12.0
                resid_ref[s, c, last, :] = (
                    resid_ref[s, c, last, :] + (16.0 * near - far)[:, lanes] / 12.0
                )

        @pl.when(other(*solver(s)))
        def _():
            give_free(s).wait_send()

        @pl.when(jnp.logical_and(other(*solver(s)), ~corner))
        def _():
            give_medium(s).wait_send()

        for axis in range(2):
            @pl.when(has_prev[axis])
            def _():
                backward(s, axis).wait_send()
        return 0

    lax.fori_loop(0, count, close, 0)


    @pl.when(solves)
    def _():
        @pl.when(line_has_next[0])
        def _():
            pass_x.wait_send()

        def settle(k, _):
            @pl.when(other(*home(k)))
            def _():
                give_home(k).wait_send()

            @pl.when(line_has_next[1])
            def _():
                pass_y(k).wait_send()

                @pl.when(other(*side(k)))
                def _():
                    pass_side(k).wait_send()
            return 0

        lax.fori_loop(0, group, settle, 0)


def staged(sizes, inputs, *refs):
    sources, refs = refs[:inputs], refs[inputs:]
    wave, resid, refs = refs[0], refs[1], refs[2:]
    targets, refs = refs[:inputs], refs[inputs:]
    in_sem, refs = refs[0], refs[1:]

    def load_inputs():
        copies = [
            pltpu.make_async_copy(source, target, in_sem.at[i])
            for i, (source, target) in enumerate(zip(sources, targets))
        ]
        for copy in copies:
            copy.start()
        for copy in copies:
            copy.wait()

    kernel(load_inputs, *sizes, *targets, wave, resid, *refs)


def solution(mesh):
    grid_rows, grid_cols = mesh.shape["gx"], mesh.shape["gy"]
    group = 8

    def body(right_side, slowness, source_cells, source_amplitudes):
        count, parts, size_x, size_y, size_z = right_side.shape
        rows = size_x * size_y
        wide = 2 * size_z
        tables = build_tables(size_x, size_y, size_z)
        dma = pltpu.SemaphoreType.DMA

        def field(*lead):
            return pltpu.VMEM((*lead, 2, rows, size_z), F32)

        def traces(*lead):
            return pltpu.VMEM((*lead, 2 * size_y, wide), F32)

        whole = pl.BlockSpec(memory_space=pl.ANY)
        block = jax.ShapeDtypeStruct((count, parts, rows, size_z), F32)
        operands = (
            right_side.reshape(count, parts, rows, size_z),
            slowness.reshape(rows, size_z),
            source_cells,
            source_amplitudes.transpose(0, 2, 1),
            *[jnp.asarray(t) for t in tables],
        )
        sizes = (grid_rows, grid_cols, (size_x, size_y, size_z), group)
        wave, resid = pl.pallas_call(
            functools.partial(staged, sizes, len(operands)),
            out_shape=(pltpu.VMEM(block.shape, F32), pltpu.VMEM(block.shape, F32)),
            in_specs=[whole] * len(operands),
            out_specs=(pl.BlockSpec(memory_space=pltpu.VMEM),) * 2,
            scratch_shapes=[pltpu.VMEM(o.shape, o.dtype) for o in operands]
            + [dma((len(operands),))]
            + [
                field(count),
                field(count),
                field(count),
                pltpu.VMEM((rows, size_z), F32),
                field(),
                traces(count, 2),
                traces(count, 2),
                traces(count),
                pltpu.VMEM((count, 2, size_x, wide), F32),
                traces(count),
                pltpu.VMEM((count, 2, size_x, wide), F32),
                pltpu.VMEM((group, rows, size_z), F32),
                traces(group, 2),
                traces(group + 1),
                traces(group),
                traces(group),
                field(),
                field(),
                field(),
                dma((count,)),
                dma((group,)),
                dma((count,)),
                dma((group,)),
                dma((group, 2)),
                dma((count, 2)),
                dma,
                dma,
                dma((group,)),
                dma((group,)),
                dma((count, 2)),
                dma((count, 2)),
            ],
            compiler_params=pltpu.CompilerParams(collective_id=0, has_side_effects=True),
        )(*operands)
        shape = (count, parts, size_x, size_y, size_z)
        return (wave.reshape(shape), resid.reshape(shape))

    return jax.shard_map(
        body,
        mesh=mesh,
        in_specs=(P(None, None, "gx", "gy", None), P("gx", "gy", None), P(), P()),
        out_specs=(P(None, None, "gx", "gy", None), P(None, None, "gx", "gy", None)),
        check_vma=False,
    )
```
